768 devices in a mesh: sec: 4 (over y_lo), dp: 48 (over y_hi, z, core), mp: 4 (over x).
Axes of the slice: x: 4, y: 8 (y_hi: 2, y_lo: 4; y = y_hi * 4 + y_lo), z: 12, core: 2. Of those that a mesh axis runs over, the one named last changes fastest.
Arguments:
- policy_query: bfloat16 [192, 128, 4096], P(('sec', 'dp'), None, 'mp'), may hold values from -6 to 6
- policy_memory: bfloat16 [2, 192, 128, 1024], P(None, ('sec', 'dp'), None, 'mp'), may hold values from -6 to 6
- chosen_output_rows: bfloat16 [192, 128, 4096], P(('sec', 'dp'), None, 'mp'), may hold values from -0.09375 to 0.09375
- adapter_rows: bfloat16 [192, 128, 8192], P(('sec', 'dp'), None, 'mp'), may hold values from -6 to 6
- adapter_down: bfloat16 [4096, 64], P('mp'), may hold values from -0.09375 to 0.09375
- adapter_up: bfloat16 [64, 8192], P(None, 'mp'), may hold values from -0.0078125 to 0.0078125
- scorer_query: bfloat16 [4, 4, 48, 128, 4096], P('sec', None, 'dp', None, 'mp'), may hold values from -6 to 6
- scorer_key_values: bfloat16 [4, 2, 4, 48, 128, 1024], P('sec', None, None, 'dp', None, 'mp'), may hold values from -6 to 6
- score_heads: float32 [2, 4096], P(None, 'mp'), may hold values from -0.1875 to 0.1875
- document_ids: int32 [4, 48, 128], P(None, 'dp'), may hold values from 0 to 3, never falling along the last dimension, each value on 1 to 64 neighbouring positions
- prompt_lengths: int32 [4, 48, 4], P(None, 'dp'), may hold values from 1 to 31
Outputs:
- advantages: float32 [192, 128], P(('sec', 'dp'))
- query_grad: bfloat16 [192, 128, 4096], P(('sec', 'dp'), None, 'mp')
- memory_grad: bfloat16 [2, 192, 128, 1024], P(None, ('sec', 'dp'), None, 'mp')
- down_grad: float32 [4096, 64], P('mp')
- up_grad: float32 [64, 8192], P(None, 'mp')
The draws below stay inside these ranges and needn't reach their ends.
Inputs may be any that keep to these rules, and one draw needn't show every extreme that they name: `document_ids`: within each row the document numbers never fall; every document has 1 to 64 positions and one has exactly 64.
All inputs are finite; a program needn't handle non-finite values.
Results may differ from the reference program's by a relative error of at most 0.0081.
Values may be sent and summed in bfloat16 or wider, within the bound.
No kernel may reach another device: no remote copies, remote signals or barrier semaphores. Data moves between devices by JAX's collectives and lax.ppermute only.
A program may use at most 32 MiB of HBM per device.

```python
import math
import jax
import jax.numpy as jnp
import numpy as np
from jax import lax

D = 8192
HEAD_DIM = 128
RANK = 64
DOCS = 4
ROW_TOKENS = 128
SECTIONS = 4
DP_ROWS = 48
PACKED_ROWS = 192
HQ = 4096
KEY_FEATURES = 1024


def draw_policy_query(key, part):
    shape = (PACKED_ROWS, ROW_TOKENS, HQ)
    return jnp.clip(jax.random.normal(jax.random.fold_in(key, 101), shape, jnp.float32), -6.0, 6.0).astype(jnp.bfloat16)


def draw_policy_memory(key, part):
    shape = (2, PACKED_ROWS, ROW_TOKENS, KEY_FEATURES)
    return jnp.clip(jax.random.normal(jax.random.fold_in(key, 202), shape, jnp.float32), -6.0, 6.0).astype(jnp.bfloat16)


def draw_scorer_query(key, part):
    shape = (SECTIONS, SECTIONS, DP_ROWS, ROW_TOKENS, HQ)
    return jnp.clip(jax.random.normal(jax.random.fold_in(key, 303), shape, jnp.float32), -6.0, 6.0).astype(jnp.bfloat16)


def draw_scorer_key_values(key, part):
    shape = (SECTIONS, 2, SECTIONS, DP_ROWS, ROW_TOKENS, KEY_FEATURES)
    return jnp.clip(jax.random.normal(jax.random.fold_in(key, 404), shape, jnp.float32), -6.0, 6.0).astype(jnp.bfloat16)


def touch_ends(array, own_key, low, high):
    place = [jax.random.randint(jax.random.fold_in(own_key, axis), (), 0, length) for axis, length in enumerate(array.shape)]
    main_axis = array.shape.index(max(array.shape))
    neighbour = place[:main_axis] + [(place[main_axis] + 1) % array.shape[main_axis]] + place[main_axis + 1:]
    return array.at[tuple(place)].set(low).at[tuple(neighbour)].set(high)


def block_levels(rng, dims, pieces, low, top_value):
    factor_of, own = 1.0, jax.random.fold_in(rng, 6)
    for dim, parts in pieces:
        steps = jnp.exp(jax.random.uniform(jax.random.fold_in(own, dim), (parts,), jnp.float32, low / len(pieces), top_value / len(pieces)))
        factor_of = factor_of * jnp.repeat(steps, dims[dim] // parts).reshape([-1 if axis == dim else 1 for axis in range(len(dims))])
    return factor_of


def profile(count, total, bound, lean):
    loads = [(1 << 20) // math.isqrt(rank ** lean) + 1 for rank in range(2, count + 1)]
    surplus, given = total - bound - (count - 1), [1] * (count - 1)
    while surplus > 0:
        candidates = [i for i in range(count - 1) if given[i] < bound]
        pool, remaining = sum([loads[i] for i in candidates]), surplus
        for i in candidates:
            extra = min(bound - given[i], max(1, remaining * loads[i] // pool), surplus)
            given[i] = given[i] + extra
            surplus = surplus - extra
    return np.array([bound] + given)


def uneven(stream_key, count, total, reach, slope):
    if count == 2:
        one = jax.random.randint(stream_key, (), max(1, total - reach), min(reach, total - 1) + 1)
        return jnp.stack([one, total - one])
    lengths = jnp.asarray(profile(count, total, reach, slope), jnp.int32)
    couples = (count - 1) // 2
    giver, receiver = lengths[1:1 + 2 * couples:2], lengths[2:2 + 2 * couples:2]
    room = jnp.minimum(giver - 1, reach - receiver)
    moved = jax.random.randint(jax.random.fold_in(stream_key, 1), (couples,), 0, 1 << 20) % (room + 1)
    lengths = lengths.at[1:1 + 2 * couples:2].set(giver - moved).at[2:2 + 2 * couples:2].set(receiver + moved)
    return lengths[jax.random.permutation(jax.random.fold_in(stream_key, 2), count)]


def scatter_about(key, extent, scale, reach, split=(), held_as=jnp.bfloat16):
    gain = block_levels(key, extent, split, -0.22, 0.18) if split else 1.0
    values = jax.random.normal(key, extent, jnp.float32) * scale * gain
    return jnp.minimum(jnp.maximum(values, -reach), reach).astype(held_as)


def setup_inputs(seed: int = 0) -> dict:
    streams_of = jax.random.split(jax.random.key(seed), 12)
    policy_query = draw_policy_query(jax.random.fold_in(streams_of[11], 71), 0)
    policy_memory = draw_policy_memory(jax.random.fold_in(streams_of[11], 71), 0)
    chosen_output_rows = scatter_about(streams_of[2], (PACKED_ROWS, ROW_TOKENS, HQ), HQ ** -0.5, 0.09375, ((0, 192), (2, 4)))
    adapter_rows = scatter_about(streams_of[3], (PACKED_ROWS, ROW_TOKENS, D), 1.0, 6.0, ((0, 192), (2, 4)))
    adapter_down = scatter_about(streams_of[4], (HQ, RANK), HQ ** -0.5, 0.09375, ((0, 4),))
    adapter_up = scatter_about(streams_of[5], (RANK, D), (D * RANK) ** -0.5, 0.0078125, ((1, 4),))
    scorer_query = draw_scorer_query(jax.random.fold_in(streams_of[11], 71), 0)
    scorer_key_values = draw_scorer_key_values(jax.random.fold_in(streams_of[11], 71), 0)
    score_heads = scatter_about(streams_of[8], (2, HQ), (HQ // 4) ** -0.5, 0.1875, ((1, 4),), jnp.float32)
    document_ids = jax.vmap(lambda own: jnp.searchsorted(jnp.cumsum(uneven(own, DOCS, ROW_TOKENS, ROW_TOKENS // 2, 0)), jnp.arange(ROW_TOKENS), side="right"))(jax.random.split(streams_of[9], SECTIONS * DP_ROWS)).reshape((SECTIONS, DP_ROWS, ROW_TOKENS)).astype(jnp.int32)
    prompt_lengths = touch_ends(jax.random.randint(streams_of[10], (SECTIONS, DP_ROWS, DOCS), 1, ROW_TOKENS // 4), jax.random.fold_in(streams_of[10], 1), 1, (ROW_TOKENS // 4) - 1).astype(jnp.int32)
    return {"policy_query": policy_query, "policy_memory": policy_memory, "chosen_output_rows": chosen_output_rows, "adapter_rows": adapter_rows, "adapter_down": adapter_down, "adapter_up": adapter_up, "scorer_query": scorer_query, "scorer_key_values": scorer_key_values, "score_heads": score_heads, "document_ids": document_ids, "prompt_lengths": prompt_lengths}


kl_weight = 0.1
trace_decay = 0.95
epsilon = 1e-05
masked_score = -1e+30

def span_masks(document_index, prompt):
    length = document_index.shape[-1]
    labels = jnp.arange(prompt.shape[-1], dtype=jnp.int32)
    member = (document_index[:, None] == labels[None, :]).astype(jnp.float32)
    counts = lax.optimization_barrier(jnp.sum(member, axis=0))
    firsts = jnp.cumsum(counts) - counts
    position = jnp.arange(length).astype(jnp.float32)
    start_pos = lax.optimization_barrier(jnp.sum(member * firsts[None, :], axis=1))
    prompt_pos = lax.optimization_barrier(jnp.sum(member * prompt.astype(jnp.float32)[None, :], axis=1))
    ending = lax.optimization_barrier(jnp.sum(member * (firsts + counts - 1.0)[None, :], axis=1))
    respond = (position - start_pos >= prompt_pos).astype(jnp.float32)
    closing = (position == ending).astype(jnp.float32)
    return (respond, closing)

def trace_matrix(document_index):
    length = document_index.shape[-1]
    position = jnp.arange(length, dtype=jnp.int32)
    later = position[None, :] - position[:, None]
    linked = (document_index[:, None] == document_index[None, :]) & (later >= 0)
    powers = jnp.power(jnp.float32(trace_decay), jnp.maximum(later, 0).astype(jnp.float32))
    return jnp.where(linked, powers, jnp.float32(0.0))

def attend_section(query, keys, values, document_index):
    length = query.shape[0]
    kv_heads = keys.shape[1] // HEAD_DIM
    groups = query.shape[1] // keys.shape[1]
    query_h = query.reshape(length, kv_heads, groups, HEAD_DIM).astype(jnp.float32)
    keys_h = keys.reshape(length, kv_heads, HEAD_DIM).astype(jnp.float32)
    values_h = values.reshape(length, kv_heads, HEAD_DIM).astype(jnp.float32)
    scores = jnp.einsum('qcgd,kcd->cgqk', query_h, keys_h) * HEAD_DIM ** (-0.5)
    position = jnp.arange(length, dtype=jnp.int32)
    allowed = (document_index[:, None] == document_index[None, :]) & (position[:, None] >= position[None, :])
    scores = jnp.where(allowed, scores, masked_score)
    top = lax.optimization_barrier(jnp.max(scores, axis=-1, keepdims=True))
    raised = jnp.exp(scores - top)
    probs = raised / lax.optimization_barrier(jnp.sum(raised, axis=-1, keepdims=True))
    probs_b = probs.astype(jnp.bfloat16)
    attended = jnp.einsum('cgqk,kcd->qcgd', probs_b.astype(jnp.float32), values_h).reshape(length, -1)
    return (attended, probs, probs_b)

def attend_back(query, keys, values, probs, probs_b, grad_b):
    length = query.shape[0]
    kv_heads = keys.shape[1] // HEAD_DIM
    groups = query.shape[1] // keys.shape[1]
    query_h = query.reshape(length, kv_heads, groups, HEAD_DIM).astype(jnp.float32)
    keys_h = keys.reshape(length, kv_heads, HEAD_DIM).astype(jnp.float32)
    values_h = values.reshape(length, kv_heads, HEAD_DIM).astype(jnp.float32)
    grad_h = grad_b.reshape(length, kv_heads, groups, HEAD_DIM).astype(jnp.float32)
    dprobs = jnp.einsum('qcgd,kcd->cgqk', grad_h, values_h)
    inner = lax.optimization_barrier(jnp.sum(probs * dprobs, axis=-1, keepdims=True))
    dscores = (probs * (dprobs - inner)).astype(jnp.bfloat16).astype(jnp.float32)
    scale = HEAD_DIM ** (-0.5)
    query_grad = (jnp.einsum('cgqk,kcd->qcgd', dscores, keys_h) * scale).astype(jnp.bfloat16).reshape(length, -1)
    keys_grad = (jnp.einsum('cgqk,qcgd->kcd', dscores, query_h) * scale).astype(jnp.bfloat16).reshape(length, -1)
    values_grad = jnp.einsum('cgqk,qcgd->kcd', probs_b.astype(jnp.float32), grad_h).astype(jnp.bfloat16).reshape(length, -1)
    return (query_grad, keys_grad, values_grad)

def reference(policy_query, policy_memory, chosen_output_rows, adapter_rows, adapter_down, adapter_up, scorer_query, scorer_key_values, score_heads, document_ids, prompt_lengths):
    highest = lax.Precision.HIGHEST
    document_list = document_ids.reshape(PACKED_ROWS, ROW_TOKENS)
    prompts = prompt_lengths.reshape(PACKED_ROWS, DOCS)
    down_float = adapter_down.astype(jnp.float32)

    def forward_row(item_list):
        query, keys, values, document_index, chosen_token, adapter = item_list
        attended, probs, probs_b = attend_section(query, keys, values, document_index)
        base = lax.optimization_barrier(jnp.sum(attended * chosen_token.astype(jnp.float32), axis=1))
        lowrank_in = jnp.dot(attended, down_float, precision=highest)
        lowrank_out = jnp.dot(adapter, adapter_up.T, preferred_element_type=jnp.float32)
        return (base, lowrank_in, lowrank_out)
    base, lowrank_in, lowrank_out = lax.map(forward_row, (policy_query, policy_memory[0], policy_memory[1], document_list, chosen_output_rows, adapter_rows))
    policy_new = base + lax.optimization_barrier(jnp.sum(lowrank_in * lowrank_out, axis=-1))
    per_section_scores = []
    for section_index in range(4):
        scorer_query_rows = scorer_query[section_index].reshape(PACKED_ROWS, ROW_TOKENS, HQ)
        scorer_keys = scorer_key_values[section_index, 0].reshape(PACKED_ROWS, ROW_TOKENS, KEY_FEATURES)
        scorer_values = scorer_key_values[section_index, 1].reshape(PACKED_ROWS, ROW_TOKENS, KEY_FEATURES)
        if section_index < 2:

            def score_row_values(item_list):
                query, keys, values, document_index, chosen_token = item_list
                attended, probs, probs_b = attend_section(query, keys, values, document_index)
                return lax.optimization_barrier(jnp.sum(attended * chosen_token.astype(jnp.float32), axis=1))
            per_section_scores.append(lax.map(score_row_values, (scorer_query_rows, scorer_keys, scorer_values, document_list, chosen_output_rows)))
        else:
            head = score_heads[section_index - 2]

            def head_row_index(item_list):
                query, keys, values, document_index = item_list
                attended, probs, probs_b = attend_section(query, keys, values, document_index)
                return jnp.dot(attended, head, precision=highest)
            per_section_scores.append(lax.map(head_row_index, (scorer_query_rows, scorer_keys, scorer_values, document_list)))
    policy_old, policy_ref, reward, value = per_section_scores
    respond, closing = jax.vmap(span_masks)(document_list, prompts)
    next_value = jnp.concatenate([value[:, 1:], jnp.zeros((PACKED_ROWS, 1), jnp.float32)], axis=1) * (1.0 - closing)
    delta = -kl_weight * (policy_old - policy_ref) + closing * reward + next_value - value
    matrices = jax.vmap(trace_matrix)(document_list)
    advantage = jnp.einsum('rtu,ru->rt', matrices, delta, precision=highest)
    count = jnp.sum(respond)
    total = jnp.sum(respond * advantage)
    square_total = jnp.sum(respond * advantage * advantage)
    mean = total / count
    spread = square_total / count - mean * mean
    whitened = respond * (advantage - mean) * lax.rsqrt(spread + epsilon)
    ratio = jnp.exp(policy_new - policy_old)
    grad_score = -respond * ratio * whitened / count

    def backward_row(carry, item_list):
        query, keys, values, document_index, chosen_token, adapter, gscore, low_in, low_out = item_list
        attended, probs, probs_b = attend_section(query, keys, values, document_index)
        scaled_out = gscore[:, None] * low_out
        grad_attended = (gscore[:, None] * chosen_token.astype(jnp.float32) + jnp.dot(scaled_out, down_float.T, precision=highest)).astype(jnp.bfloat16)
        down_term = jnp.dot(attended.T, scaled_out, precision=highest)
        scaled_in = (gscore[:, None] * low_in).astype(jnp.bfloat16)
        up_term = jnp.dot(scaled_in.T, adapter, preferred_element_type=jnp.float32)
        grads = attend_back(query, keys, values, probs, probs_b, grad_attended)
        return ((carry[0] + down_term, carry[1] + up_term), grads)
    start = (jnp.zeros((HQ, RANK), jnp.float32), jnp.zeros((RANK, D), jnp.float32))
    sums, grads = lax.scan(backward_row, start, (policy_query, policy_memory[0], policy_memory[1], document_list, chosen_output_rows, adapter_rows, grad_score, lowrank_in, lowrank_out))
    query_grad, keys_grad, values_grad = grads
    return (whitened, query_grad, jnp.stack([keys_grad, values_grad]), sums[0], sums[1])
```

```python
import functools
import jax
import jax.numpy as jnp
import numpy as np
from jax import lax
from jax.experimental import pallas as pl
from jax.experimental.pallas import tpu as pltpu
from jax.sharding import Mesh, PartitionSpec as P

HEAD = 128
KL = 0.1
DECAY = 0.95
EPS = 1e-05
MASKED = -1e30
F32 = jnp.float32
BF16 = jnp.bfloat16
NT = (((1,), (1,)), ((), ()))
NN = (((1,), (0,)), ((), ()))
TN = (((0,), (0,)), ((), ()))


def dot(a, b, dims):
    return lax.dot_general(a, b, dims, preferred_element_type=F32)


def halves(x):
    high = x.astype(BF16)
    return high, (x - high.astype(F32)).astype(BF16)


def as_column(row):
    n = row.shape[1]
    return jnp.broadcast_to(row, (n, n)).T


def square(row):
    n = row.shape[1]
    return jnp.broadcast_to(row, (n, n))


def allowed_of(doc_row):
    n = doc_row.shape[1]
    doc = doc_row.astype(F32)
    rows = lax.broadcasted_iota(jnp.int32, (n, n), 0)
    lanes = lax.broadcasted_iota(jnp.int32, (n, n), 1)
    return (as_column(doc) == square(doc)) & (rows >= lanes)


def probs_of(query, keys, allowed):
    scores = dot(query, keys, NT) * HEAD ** (-0.5)
    scores = jnp.where(allowed, scores, MASKED)
    top = jnp.max(scores, axis=1, keepdims=True)
    raised = jnp.exp(scores - top)
    return raised / jnp.sum(raised, axis=1, keepdims=True)


def scorer_kernel(doc_ref, q_ref, k_ref, v_ref, out_ref):
    allowed = allowed_of(doc_ref[...])
    groups = q_ref.shape[1] // k_ref.shape[1]
    for head in range(q_ref.shape[1] // HEAD):
        at = slice(head * HEAD, (head + 1) * HEAD)
        kv = slice(head // groups * HEAD, (head // groups + 1) * HEAD)
        probs = probs_of(q_ref[:, at], k_ref[:, kv], allowed).astype(BF16)
        out_ref[:, at] = dot(probs, v_ref[:, kv], NN)


def score_kernel(sec_ref, att_ref, rows_ref, heads_ref, out_ref):
    n_heads = att_ref.shape[2] // HEAD
    by_rows = sec_ref[0] < 2
    first_head = sec_ref[0] == 2

    def put(weight):
        for row in range(att_ref.shape[0]):
            total = None
            for head in range(n_heads):
                at = slice(head * HEAD, (head + 1) * HEAD)
                term = att_ref[row, :, at] * weight(row, at)
                total = term if total is None else total + term
            out_ref[row:row + 1, :] = jnp.sum(total.T, axis=0, keepdims=True)

    @pl.when(by_rows)
    def _():
        put(lambda row, at: rows_ref[row, :, at].astype(F32))

    @pl.when(jnp.logical_not(by_rows))
    def _():
        put(lambda row, at: jnp.where(first_head, heads_ref[0:1, at], heads_ref[1:2, at]))


def policy_kernel(sec_ref, doc_ref, q_ref, k_ref, v_ref, rows_ref, adapter_ref, down_ref, up_ref,
                  att_ref, probs_ref, part_ref):
    allowed = allowed_of(doc_ref[sec_ref[0]])
    groups = q_ref.shape[1] // k_ref.shape[1]
    base = None
    low_in = None
    for head in range(q_ref.shape[1] // HEAD):
        at = slice(head * HEAD, (head + 1) * HEAD)
        kv = slice(head // groups * HEAD, (head // groups + 1) * HEAD)
        probs = probs_of(q_ref[:, at], k_ref[:, kv], allowed)
        probs_ref[head] = probs
        attended = dot(probs.astype(BF16), v_ref[:, kv], NN)
        att_ref[:, at] = attended
        term = attended * rows_ref[:, at].astype(F32)
        base = term if base is None else base + term
        high, low = halves(attended)
        down = down_ref[:, at]
        term = dot(down, high, NT) + dot(down, low, NT)
        low_in = term if low_in is None else low_in + term
    rank = down_ref.shape[0]
    part_ref[0:rank, :] = low_in
    part_ref[rank:2 * rank, :] = dot(up_ref[...], adapter_ref[...], NT)
    base_row = jnp.sum(base.T, axis=0, keepdims=True)
    part_ref[2 * rank:, :] = jnp.broadcast_to(base_row, (8, base_row.shape[1]))


def delta_kernel(sec_ref, prompt_ref, doc_ref, part_ref, keep_ref, sums_ref):
    sec = sec_ref[0]
    doc = doc_ref[sec].astype(F32)
    n = doc.shape[1]
    doc_col, doc_row = as_column(doc), square(doc)
    rows = lax.broadcasted_iota(jnp.int32, (n, n), 0)
    lanes = lax.broadcasted_iota(jnp.int32, (n, n), 1)
    position = lax.broadcasted_iota(jnp.int32, (1, n), 1).astype(F32)
    start = jnp.sum(jnp.where(doc_col < doc_row, 1.0, 0.0), axis=0, keepdims=True)
    ending = jnp.sum(jnp.where(doc_col <= doc_row, 1.0, 0.0), axis=0, keepdims=True) - 1.0
    prompt = jnp.zeros((1, n), F32)
    for label in range(prompt_ref.shape[1]):
        length = prompt_ref[sec, label].astype(F32)
        prompt = jnp.where(doc == float(label), length, prompt)
    respond = jnp.where(position - start >= prompt, 1.0, 0.0)
    closing = jnp.where(position == ending, 1.0, 0.0)

    def section(index):
        return jnp.sum(part_ref[index], axis=0, keepdims=True)

    old, ref, reward, value = section(0), section(1), section(2), section(3)
    next_value = jnp.where(position < n - 1.0, pltpu.roll(value, n - 1, 1), 0.0) * (1.0 - closing)
    delta = -KL * (old - ref) + closing * reward + next_value - value
    later = rows - lanes
    linked = (doc_col == doc_row) & (later >= 0)
    powers = jnp.exp(jnp.maximum(later, 0).astype(F32) * float(np.log(DECAY)))
    terms = jnp.where(linked, powers, 0.0) * as_column(delta)
    advantage = jnp.sum(terms, axis=0, keepdims=True)
    keep_ref[0:1, :] = respond
    keep_ref[1:2, :] = advantage
    keep_ref[2:3, :] = old
    keep_ref[3:8, :] = jnp.zeros((5, n), F32)
    lane = lax.broadcasted_iota(jnp.int32, (1, n), 1)
    count = jnp.sum(respond, axis=1, keepdims=True)
    total = jnp.sum(respond * advantage, axis=1, keepdims=True)
    squares = jnp.sum(respond * advantage * advantage, axis=1, keepdims=True)
    packed = jnp.where(lane == 0, count, jnp.where(lane == 1, total, jnp.where(lane == 2, squares, 0.0)))
    sums_ref[...] = jnp.broadcast_to(packed, sums_ref.shape)


def weights_kernel(moments_ref, keep_ref, part_ref, att_ref, adapter_ref,
                   white_ref, grad_ref, out_ref, down_ref, up_ref):
    rank = (part_ref.shape[1] - 8) // 2
    moments = jnp.sum(moments_ref[...], axis=0, keepdims=True)
    lane = lax.broadcasted_iota(jnp.int32, moments.shape, 1)

    def pick(index):
        return jnp.sum(jnp.where(lane == index, moments, 0.0), axis=1, keepdims=True)

    count, total, squares = pick(0), pick(1), pick(2)
    mean = total / count
    spread = squares / count - mean * mean
    respond, advantage, old = keep_ref[0:1, :], keep_ref[1:2, :], keep_ref[2:3, :]
    whitened = respond * (advantage - mean) * lax.rsqrt(spread + EPS)
    white_ref[...] = whitened
    part = part_ref[0].astype(F32)
    for index in range(1, part_ref.shape[0]):
        part = part + part_ref[index].astype(F32)
    low_in, low_out, base = part[0:rank], part[rank:2 * rank], part[2 * rank:2 * rank + 1]
    policy_new = base + jnp.sum(low_in * low_out, axis=0, keepdims=True)
    grad_score = -respond * jnp.exp(policy_new - old) * whitened / count
    grad_ref[...] = grad_score
    scaled_out = grad_score * low_out
    out_ref[...] = scaled_out
    high, low = halves(scaled_out)
    att_high, att_low = halves(att_ref[...])
    down_ref[...] = dot(high, att_high, NN) + (dot(low, att_high, NN) + dot(high, att_low, NN))
    up_ref[...] = dot((grad_score * low_in).astype(BF16), adapter_ref[...], NN)


def backward_kernel(grad_ref, out_ref, down_ref, rows_ref, probs_ref, q_ref, k_ref, v_ref,
                    query_ref, keys_ref, values_ref):
    grad_col = as_column(grad_ref[...])
    high, low = halves(out_ref[...])
    groups = q_ref.shape[1] // k_ref.shape[1]
    scale = HEAD ** (-0.5)
    for group in range(k_ref.shape[1] // HEAD):
        kv = slice(group * HEAD, (group + 1) * HEAD)
        keys, values = k_ref[:, kv], v_ref[:, kv]
        keys_grad, values_grad = None, None
        for head in range(group * groups, (group + 1) * groups):
            at = slice(head * HEAD, (head + 1) * HEAD)
            down = down_ref[:, at]
            grad = grad_col * rows_ref[:, at].astype(F32) + (dot(high, down, TN) + dot(low, down, TN))
            grad = grad.astype(BF16)
            probs = probs_ref[head]
            dprobs = dot(grad, values, NT)
            inner = jnp.sum(probs * dprobs, axis=1, keepdims=True)
            dscores = (probs * (dprobs - inner)).astype(BF16)
            query_ref[:, at] = (dot(dscores, keys, NN) * scale).astype(BF16)
            term = dot(dscores, q_ref[:, at], TN)
            keys_grad = term if keys_grad is None else keys_grad + term
            term = dot(probs.astype(BF16), grad, TN)
            values_grad = term if values_grad is None else values_grad + term
        keys_ref[:, kv] = (keys_grad * scale).astype(BF16)
        values_ref[:, kv] = values_grad.astype(BF16)


def gather_moments(sums, n_sec, sizes):
    n_yh, n_z, n_core = sizes
    first = share(sums[0:1], ("z", "core"), n_z * n_core).sum(axis=0)
    return share(first, ("sec", "yh"), n_sec * n_yh).reshape(-1, sums.shape[1])


def reduce_grads(down_part, up_part, n_sec, sizes):
    n_yh, n_z, n_core = sizes
    n_y = n_sec * n_yh
    tokens = 128
    flat = jnp.concatenate([down_part.reshape(-1, tokens), up_part.reshape(-1, tokens)], axis=0)
    total = flat.shape[0]
    x = flat.reshape(n_core, total // n_core, tokens)
    x = reduce_part(x, "core", n_core)
    x = reduce_part(x.reshape(n_z, -1, tokens), "z", n_z)
    x = reduce_part(x.reshape(n_y, -1, tokens), ("sec", "yh"), n_y)
    x = share(x, ("sec", "yh"), n_y).reshape(-1, tokens)
    x = share(x, "z", n_z).reshape(-1, tokens)
    x = share(x, "core", n_core).reshape(total, tokens)
    cut = down_part.size // tokens
    return x[:cut].reshape(down_part.shape), x[cut:].reshape(up_part.shape)


def whole(shape, space=pltpu.VMEM):
    return pl.BlockSpec(memory_space=space)


def call(kernel, outs, args, smem=(), **params):
    specs = [pl.BlockSpec(memory_space=pltpu.SMEM if i in smem else pltpu.VMEM) for i in range(len(args))]
    return pl.pallas_call(
        kernel,
        out_shape=outs,
        in_specs=specs,
        out_specs=jax.tree.map(lambda _: pl.BlockSpec(memory_space=pltpu.VMEM), outs),
        interpret=INTERPRET,
        **params,
    )(*args)


def sds(shape, dtype=F32):
    return jax.ShapeDtypeStruct(shape, dtype)


INTERPRET = False
SPLIT = (2, 12, 2)
AXES = ("sec", "yh", "z", "core", "mp")
DP = ("yh", "z", "core")


def share(x, axes, n):
    return lax.all_to_all(jnp.broadcast_to(x[None], (n,) + x.shape), axes, 0, 0, tiled=True)


def reduce_part(x, axes, n):
    got = lax.all_to_all(x, axes, 0, 0, tiled=True)
    return jnp.sum(got, axis=0)


def on_device(policy_query, policy_memory, chosen, adapter_rows, adapter_down, adapter_up,
              scorer_query, scorer_key_values, score_heads, document_ids, prompt_lengths):
    sec = lax.axis_index("sec").astype(jnp.int32).reshape(1)
    n_sec, n_mp = lax.axis_size("sec"), lax.axis_size("mp")
    sizes = [lax.axis_size(a) for a in DP]
    query, keys, values = policy_query[0], policy_memory[0, 0], policy_memory[1, 0]
    rows = chosen[0]
    tokens, features = query.shape
    kv_features = keys.shape[1]
    adapter = adapter_rows[0]
    down = adapter_down.T
    rank = down.shape[0]
    width = adapter.shape[1]
    heads = features // HEAD
    prompts = prompt_lengths[:, 0]

    rows_all = lax.all_gather(rows, "sec", axis=0, tiled=False)
    scorer_att = pl.pallas_call(
        scorer_kernel,
        grid=(n_sec,),
        out_shape=sds((n_sec, tokens, features)),
        in_specs=[
            pl.BlockSpec((None, 1, tokens), lambda j: (j, 0, 0)),
            pl.BlockSpec((None, None, None, tokens, features), lambda j: (0, j, 0, 0, 0)),
            pl.BlockSpec((None, None, None, None, tokens, kv_features), lambda j: (0, 0, j, 0, 0, 0)),
            pl.BlockSpec((None, None, None, None, tokens, kv_features), lambda j: (0, 1, j, 0, 0, 0)),
        ],
        out_specs=pl.BlockSpec((None, tokens, features), lambda j: (j, 0, 0)),
        interpret=INTERPRET,
        cost_estimate=pl.CostEstimate(flops=300_000_000, bytes_accessed=5_000_000, transcendentals=600_000),
    )(document_ids, scorer_query, scorer_key_values, scorer_key_values)
    attended, probs, part = call(
        policy_kernel,
        (sds((tokens, features)), sds((heads, tokens, tokens)), sds((2 * rank + 8, tokens))),
        (sec, document_ids, query, keys, values, rows, adapter, down, adapter_up),
        smem=(0,),
        cost_estimate=pl.CostEstimate(flops=150_000_000, bytes_accessed=3_000_000, transcendentals=150_000),
    )
    parts = share(part, "mp", n_mp)
    partials = call(score_kernel, sds((n_sec, tokens)), (sec, scorer_att, rows_all, score_heads), smem=(0,),
                    cost_estimate=pl.CostEstimate(flops=2_000_000, bytes_accessed=3_000_000, transcendentals=0))
    sent = jnp.broadcast_to(partials[:, None], (n_sec, n_mp, tokens)).reshape(n_sec * n_mp, 1, tokens)
    got = lax.all_to_all(sent, ("sec", "mp"), 0, 0, tiled=True).reshape(n_sec, n_mp, tokens)
    keep, sums = call(delta_kernel, (sds((8, tokens)), sds((8, tokens))),
                      (sec, prompts, document_ids, got), smem=(0, 1))
    moments = gather_moments(sums, n_sec, sizes)
    white, grad_score, scaled_out, down_part, up_part = call(
        weights_kernel,
        (sds((1, tokens)), sds((1, tokens)), sds((rank, tokens)), sds((rank, features)), sds((rank, width))),
        (moments, keep, parts, attended, adapter),
    )
    down_grad, up_grad = reduce_grads(down_part, up_part, n_sec, sizes)
    query_grad, keys_grad, values_grad = call(
        backward_kernel,
        (sds((tokens, features), BF16), sds((tokens, kv_features), BF16), sds((tokens, kv_features), BF16)),
        (grad_score, scaled_out, down, rows, probs, query, keys, values),
        cost_estimate=pl.CostEstimate(flops=300_000_000, bytes_accessed=4_000_000, transcendentals=0),
    )
    memory_grad = jnp.stack([keys_grad, values_grad])[:, None]
    return white, query_grad[None], memory_grad, down_grad.T, up_grad


def solution(mesh):
    devices = mesh.devices
    split = SPLIT if int(np.prod(SPLIT)) == devices.shape[1] else (1, devices.shape[1], 1)
    inner = Mesh(devices.reshape((devices.shape[0],) + split + (devices.shape[2],)), AXES)
    both = ("sec",) + DP
    return jax.shard_map(
        on_device,
        mesh=inner,
        in_specs=(
            P(both, None, "mp"),
            P(None, both, None, "mp"),
            P(both, None, "mp"),
            P(both, None, "mp"),
            P("mp", None),
            P(None, "mp"),
            P("sec", None, DP, None, "mp"),
            P("sec", None, None, DP, None, "mp"),
            P(None, "mp"),
            P(None, DP, None),
            P(None, DP, None),
        ),
        out_specs=(
            P(both, None),
            P(both, None, "mp"),
            P(None, both, None, "mp"),
            P("mp", None),
            P(None, "mp"),
        ),
        check_vma=False,
    )
```

```python
import jax
import jax.numpy as jnp
import numpy as np
from jax import lax
from jax.experimental import pallas as pl
from jax.experimental.pallas import tpu as pltpu
from jax.sharding import Mesh, PartitionSpec as P

HEAD = 128
KL = 0.1
DECAY = 0.95
EPS = 1e-05
MASKED = -1e30
F32 = jnp.float32
BF16 = jnp.bfloat16
NT = (((1,), (1,)), ((), ()))
NN = (((1,), (0,)), ((), ()))
TN = (((0,), (0,)), ((), ()))


def dot(a, b, dims):
    return lax.dot_general(a, b, dims, preferred_element_type=F32)


def halves(x):
    high = x.astype(BF16)
    return high, (x - high.astype(F32)).astype(BF16)


def as_column(row):
    n = row.shape[1]
    return jnp.broadcast_to(row, (n, n)).T


def square(row):
    n = row.shape[1]
    return jnp.broadcast_to(row, (n, n))


def allowed_of(doc_row):
    n = doc_row.shape[1]
    doc = doc_row.astype(F32)
    rows = lax.broadcasted_iota(jnp.int32, (n, n), 0)
    lanes = lax.broadcasted_iota(jnp.int32, (n, n), 1)
    return (as_column(doc) == square(doc)) & (rows >= lanes)


def probs_of(query, keys, allowed):
    scores = dot(query, keys, NT) * HEAD ** (-0.5)
    scores = jnp.where(allowed, scores, MASKED)
    top = jnp.max(scores, axis=1, keepdims=True)
    raised = jnp.exp(scores - top)
    return raised / jnp.sum(raised, axis=1, keepdims=True)


def scorer_kernel(doc_ref, q_ref, k_ref, v_ref, after_ref, out_ref):
    del after_ref
    allowed = allowed_of(doc_ref[...])
    groups = q_ref.shape[1] // k_ref.shape[1]
    for head in range(q_ref.shape[1] // HEAD):
        at = slice(head * HEAD, (head + 1) * HEAD)
        kv = slice(head // groups * HEAD, (head // groups + 1) * HEAD)
        probs = probs_of(q_ref[:, at], k_ref[:, kv], allowed).astype(BF16)
        out_ref[:, at] = dot(probs, v_ref[:, kv], NN)


def score_kernel(sec_ref, att_ref, own_ref, next_ref, after_ref, last_ref, heads_ref, out_ref):
    sec = sec_ref[0]
    n_sec = att_ref.shape[0]
    copies = out_ref.shape[0] // n_sec
    n_heads = att_ref.shape[2] // HEAD
    held = (own_ref, next_ref, after_ref, last_ref)

    def put(weight):
        for step in range(n_sec):
            row = lax.rem(sec + step, n_sec)
            total = None
            for head in range(n_heads):
                at = slice(head * HEAD, (head + 1) * HEAD)
                term = att_ref[row, :, at] * weight(step, at)
                total = term if total is None else total + term
            score = jnp.sum(total.T, axis=0, keepdims=True)
            for copy in range(copies):
                out_ref[row * copies + copy] = score

    @pl.when(sec < 2)
    def _():
        put(lambda step, at: held[step][:, at].astype(F32))

    @pl.when(sec >= 2)
    def _():
        put(lambda step, at: jnp.where(sec == 2, heads_ref[0:1, at], heads_ref[1:2, at]))


def policy_kernel(sec_ref, doc_ref, q_ref, memory_ref, rows_ref, adapter_ref, down_ref, up_ref,
                  att_ref, probs_ref, part_ref):
    k_ref, v_ref = memory_ref.at[0, 0], memory_ref.at[1, 0]
    allowed = allowed_of(doc_ref[sec_ref[0]])
    groups = q_ref.shape[1] // k_ref.shape[1]
    base = None
    low_in = None
    for head in range(q_ref.shape[1] // HEAD):
        at = slice(head * HEAD, (head + 1) * HEAD)
        kv = slice(head // groups * HEAD, (head // groups + 1) * HEAD)
        probs = probs_of(q_ref[:, at], k_ref[:, kv], allowed)
        probs_ref[head] = probs
        attended = dot(probs.astype(BF16), v_ref[:, kv], NN)
        att_ref[:, at] = attended
        term = attended * rows_ref[:, at].astype(F32)
        base = term if base is None else base + term
        high, low = halves(attended)
        down = down_ref[:, at]
        term = dot(down, high, NT) + dot(down, low, NT)
        low_in = term if low_in is None else low_in + term
    rank = down_ref.shape[0]
    part_ref[0:rank, :] = low_in
    part_ref[rank:2 * rank, :] = dot(up_ref[...], adapter_ref[...], NT)
    base_row = jnp.sum(base.T, axis=0, keepdims=True)
    part_ref[2 * rank:, :] = jnp.broadcast_to(base_row, (8, base_row.shape[1]))


def delta_kernel(sec_ref, prompt_ref, doc_ref, part_ref, keep_ref, sums_ref):
    sec = sec_ref[0]
    doc = doc_ref[sec].astype(F32)
    n = doc.shape[1]
    doc_col, doc_row = as_column(doc), square(doc)
    rows = lax.broadcasted_iota(jnp.int32, (n, n), 0)
    lanes = lax.broadcasted_iota(jnp.int32, (n, n), 1)
    position = lax.broadcasted_iota(jnp.int32, (1, n), 1).astype(F32)
    start = jnp.sum(jnp.where(doc_col < doc_row, 1.0, 0.0), axis=0, keepdims=True)
    ending = jnp.sum(jnp.where(doc_col <= doc_row, 1.0, 0.0), axis=0, keepdims=True) - 1.0
    prompt = jnp.zeros((1, n), F32)
    for label in range(prompt_ref.shape[1]):
        length = prompt_ref[sec, label].astype(F32)
        prompt = jnp.where(doc == float(label), length, prompt)
    respond = jnp.where(position - start >= prompt, 1.0, 0.0)
    closing = jnp.where(position == ending, 1.0, 0.0)

    def section(index):
        return jnp.sum(part_ref[index], axis=0, keepdims=True)

    old, ref, reward, value = section(0), section(1), section(2), section(3)
    next_value = jnp.where(position < n - 1.0, pltpu.roll(value, n - 1, 1), 0.0) * (1.0 - closing)
    delta = -KL * (old - ref) + closing * reward + next_value - value
    later = rows - lanes
    linked = (doc_col == doc_row) & (later >= 0)
    powers = jnp.exp(jnp.maximum(later, 0).astype(F32) * float(np.log(DECAY)))
    terms = jnp.where(linked, powers, 0.0) * as_column(delta)
    advantage = jnp.sum(terms, axis=0, keepdims=True)
    keep_ref[0:1, :] = respond
    keep_ref[1:2, :] = advantage
    keep_ref[2:3, :] = old
    keep_ref[3:8, :] = jnp.zeros((5, n), F32)
    lane = lax.broadcasted_iota(jnp.int32, (1, n), 1)
    count = jnp.sum(respond, axis=1, keepdims=True)
    total = jnp.sum(respond * advantage, axis=1, keepdims=True)
    squares = jnp.sum(respond * advantage * advantage, axis=1, keepdims=True)
    packed = jnp.where(lane == 0, count, jnp.where(lane == 1, total, jnp.where(lane == 2, squares, 0.0)))
    for copy in range(sums_ref.shape[0]):
        sums_ref[copy] = packed


def weights_kernel(core_ref, moments_ref, keep_ref, att_ref, adapter_ref, part0, part1, part2, part3,
                   white_ref, grad_ref, out_ref, own_ref, send_ref, both_ref):
    rank = (part0.shape[0] - 8) // 2
    moments = jnp.sum(moments_ref[...], axis=0, keepdims=True)
    lane = lax.broadcasted_iota(jnp.int32, moments.shape, 1)

    def pick(index):
        return jnp.sum(jnp.where(lane == index, moments, 0.0), axis=1, keepdims=True)

    count, total, squares = pick(0), pick(1), pick(2)
    mean = total / count
    spread = squares / count - mean * mean
    respond, advantage, old = keep_ref[0:1, :], keep_ref[1:2, :], keep_ref[2:3, :]
    whitened = respond * (advantage - mean) * lax.rsqrt(spread + EPS)
    white_ref[...] = whitened
    part = (part0[...] + part1[...]) + (part2[...] + part3[...])
    low_in, low_out, base = part[0:rank], part[rank:2 * rank], part[2 * rank:2 * rank + 1]
    policy_new = base + jnp.sum(low_in * low_out, axis=0, keepdims=True)
    grad_score = -respond * jnp.exp(policy_new - old) * whitened / count
    grad_ref[...] = grad_score
    scaled_out = grad_score * low_out
    out_ref[...] = scaled_out
    high, low = halves(scaled_out)
    scaled_in = (grad_score * low_in).astype(BF16)
    n_down = att_ref.shape[1] // HEAD
    for block in range(both_ref.shape[0]):
        if block < n_down:
            att_high, att_low = halves(att_ref[:, block * HEAD:(block + 1) * HEAD])
            value = dot(high, att_high, NN) + (dot(low, att_high, NN) + dot(high, att_low, NN))
        else:
            at = (block - n_down) * HEAD
            value = dot(scaled_in, adapter_ref[:, at:at + HEAD], NN)
        both_ref[block] = value
    core = core_ref[0]
    cores = both_ref.shape[0] // own_ref.shape[0]
    for slot in range(own_ref.shape[0]):
        own_ref[slot] = both_ref[core * own_ref.shape[0] + slot]
        send_ref[slot] = both_ref[(cores - 1 - core) * own_ref.shape[0] + slot]


def spread_kernel(got_ref, out_ref):
    total = got_ref[0].astype(F32)
    for index in range(1, got_ref.shape[0]):
        total = total + got_ref[index].astype(F32)
    total = total.astype(BF16)
    for index in range(out_ref.shape[0]):
        out_ref[index] = total


def place_kernel(core_ref, own_ref, other_ref, down_ref, up_ref, both_ref):
    core = core_ref[0]
    slots = own_ref.shape[0]
    cores = both_ref.shape[0] // slots
    for slot in range(slots):
        both_ref[(cores - 1 - core) * slots + slot] = other_ref[slot]
        both_ref[core * slots + slot] = own_ref[slot]
    n_down = down_ref.shape[1] // HEAD
    for block in range(both_ref.shape[0]):
        value = both_ref[block].astype(F32)
        if block < n_down:
            down_ref[:, block * HEAD:(block + 1) * HEAD] = value
        else:
            at = (block - n_down) * HEAD
            up_ref[:, at:at + HEAD] = value


def backward_kernel(grad_ref, out_ref, down_ref, rows_ref, probs_ref, q_ref, memory_ref,
                    query_ref, memory_grad_ref):
    k_ref, v_ref = memory_ref.at[0, 0], memory_ref.at[1, 0]
    grad_col = as_column(grad_ref[...])
    high, low = halves(out_ref[...])
    groups = q_ref.shape[1] // k_ref.shape[1]
    scale = HEAD ** (-0.5)
    for group in range(k_ref.shape[1] // HEAD):
        kv = slice(group * HEAD, (group + 1) * HEAD)
        keys, values = k_ref[:, kv], v_ref[:, kv]
        keys_grad, values_grad = None, None
        for head in range(group * groups, (group + 1) * groups):
            at = slice(head * HEAD, (head + 1) * HEAD)
            down = down_ref[:, at]
            grad = grad_col * rows_ref[:, at].astype(F32) + (dot(high, down, TN) + dot(low, down, TN))
            grad = grad.astype(BF16)
            probs = probs_ref[head]
            dprobs = dot(grad, values, NT)
            inner = jnp.sum(probs * dprobs, axis=1, keepdims=True)
            dscores = (probs * (dprobs - inner)).astype(BF16)
            query_ref[:, at] = (dot(dscores, keys, NN) * scale).astype(BF16)
            term = dot(dscores, q_ref[:, at], TN)
            keys_grad = term if keys_grad is None else keys_grad + term
            term = dot(probs.astype(BF16), grad, TN)
            values_grad = term if values_grad is None else values_grad + term
        memory_grad_ref[0, 0, :, kv] = (keys_grad * scale).astype(BF16)
        memory_grad_ref[1, 0, :, kv] = values_grad.astype(BF16)


def call(kernel, outs, args, smem=(), scratch=(), **params):
    specs = [pl.BlockSpec(memory_space=pltpu.SMEM if i in smem else pltpu.VMEM) for i in range(len(args))]
    return pl.pallas_call(
        kernel,
        out_shape=outs,
        in_specs=specs,
        out_specs=jax.tree.map(lambda _: pl.BlockSpec(memory_space=pltpu.VMEM), outs),
        scratch_shapes=scratch,
        interpret=INTERPRET,
        **params,
    )(*args)


def sds(shape, dtype=F32):
    return jax.ShapeDtypeStruct(shape, dtype)


INTERPRET = False
SPLIT = (2, 12, 2)
AXES = ("sec", "yh", "z", "core", "mp")
DP = ("yh", "z", "core")
Y = ("sec", "yh")


def share(x, axes, n):
    return exchange(jnp.broadcast_to(x[None], (n,) + x.shape), axes)


def exchange(x, axes):
    return lax.all_to_all(x, axes, 0, 0, tiled=True)


def swap(x, n):
    return lax.ppermute(x, "core", [(i, n - 1 - i) for i in range(n)])


def on_device(policy_query, policy_memory, chosen, adapter_rows, adapter_down, adapter_up,
              scorer_query, scorer_key_values, score_heads, document_ids, prompt_lengths):
    sec = lax.axis_index("sec").astype(jnp.int32).reshape(1)
    core = lax.axis_index("core").astype(jnp.int32).reshape(1)
    n_sec, n_mp = lax.axis_size("sec"), lax.axis_size("mp")
    n_yh, n_z, n_core = (lax.axis_size(a) for a in DP)
    n_y = n_sec * n_yh
    query = policy_query[0]
    rows = chosen[0]
    tokens, features = query.shape
    kv_features = policy_memory.shape[3]
    adapter = adapter_rows[0]
    down = adapter_down.T
    rank = down.shape[0]
    width = adapter.shape[1]
    heads = features // HEAD
    prompts = prompt_lengths[:, 0]
    blocks = (features + width) // HEAD
    half = sds((blocks // n_core, rank, HEAD))

    held = (
        rows,
        lax.ppermute(rows, "sec", [(1, 0), (2, 1)]),
        lax.ppermute(rows, "sec", [(2, 0), (3, 1)]),
        lax.ppermute(rows, "sec", [(3, 0), (0, 1)]),
    )
    attended, probs, part = call(
        policy_kernel,
        (sds((tokens, features)), sds((heads, tokens, tokens)), sds((2 * rank + 8, tokens))),
        (sec, document_ids, query, policy_memory, rows, adapter, down, adapter_up),
        smem=(0,),
        cost_estimate=pl.CostEstimate(flops=150_000_000, bytes_accessed=3_000_000, transcendentals=150_000),
    )
    parts = (part,) + tuple(
        lax.ppermute(part, "mp", [(i, (i + k) % n_mp) for i in range(n_mp)]) for k in range(1, n_mp)
    )
    scorer = pl.pallas_call(
        scorer_kernel,
        grid=(n_sec,),
        out_shape=sds((n_sec, tokens, features)),
        in_specs=[
            pl.BlockSpec((None, 1, tokens), lambda j: (j, 0, 0)),
            pl.BlockSpec((None, None, None, tokens, features), lambda j: (0, j, 0, 0, 0)),
            pl.BlockSpec((None, None, None, None, tokens, kv_features), lambda j: (0, 0, j, 0, 0, 0)),
            pl.BlockSpec((None, None, None, None, tokens, kv_features), lambda j: (0, 1, j, 0, 0, 0)),
            pl.BlockSpec(memory_space=pl.ANY),
        ],
        out_specs=pl.BlockSpec((None, tokens, features), lambda j: (j, 0, 0)),
        interpret=INTERPRET,
        cost_estimate=pl.CostEstimate(flops=300_000_000, bytes_accessed=30_000_000, transcendentals=600_000),
    )
    scorer_att = scorer(document_ids, scorer_query, scorer_key_values, scorer_key_values, part)
    partials = call(score_kernel, sds((n_sec * n_mp, 1, tokens)), (sec, scorer_att) + held + (score_heads,),
                    smem=(0,),
                    cost_estimate=pl.CostEstimate(flops=2_000_000, bytes_accessed=3_000_000, transcendentals=0))
    got = exchange(partials, ("sec", "mp")).reshape(n_sec, n_mp, tokens)
    keep, sums = call(delta_kernel, (sds((8, tokens)), sds((n_z * n_core, 1, tokens))),
                      (sec, prompts, document_ids, got), smem=(0, 1))
    sums = exchange(sums, ("z", "core")).sum(axis=0)
    moments = share(sums, Y, n_y).reshape(n_y, tokens)
    white, grad_score, scaled_out, own, send = call(
        weights_kernel,
        (sds((1, tokens)), sds((1, tokens)), sds((rank, tokens)), half, half),
        (core, moments, keep, attended, adapter) + parts,
        smem=(0,),
        scratch=(pltpu.VMEM((blocks, rank, HEAD), F32),),
    )
    summed = own + swap(send, n_core) if n_core > 1 else own
    got = exchange(summed.astype(BF16).reshape(n_z, -1, HEAD), "z")
    per = got.shape[1]
    got = exchange(call(spread_kernel, sds((n_y, per, HEAD), BF16), (got,)), Y)
    got = exchange(call(spread_kernel, sds((n_z, per, HEAD), BF16), (got,)), "z")
    got = got.reshape(half.shape)
    down_grad, up_grad = call(place_kernel, (sds((rank, features)), sds((rank, width))),
                              (core, got, swap(got, n_core)), smem=(0,),
                              scratch=(pltpu.VMEM((blocks, rank, HEAD), BF16),))
    query_grad, memory_grad = call(
        backward_kernel,
        (sds((tokens, features), BF16), sds(policy_memory.shape, BF16)),
        (grad_score, scaled_out, down, rows, probs, query, policy_memory),
        cost_estimate=pl.CostEstimate(flops=300_000_000, bytes_accessed=20_000_000, transcendentals=0),
    )
    return white, query_grad[None], memory_grad, down_grad.T, up_grad


def solution(mesh):
    devices = mesh.devices
    split = SPLIT if int(np.prod(SPLIT)) == devices.shape[1] else (1, devices.shape[1], 1)
    inner = Mesh(devices.reshape((devices.shape[0],) + split + (devices.shape[2],)), AXES)
    both = ("sec",) + DP

    return jax.shard_map(
        on_device,
        mesh=inner,
        in_specs=(
            P(both, None, "mp"),
            P(None, both, None, "mp"),
            P(both, None, "mp"),
            P(both, None, "mp"),
            P("mp", None),
            P(None, "mp"),
            P("sec", None, DP, None, "mp"),
            P("sec", None, None, DP, None, "mp"),
            P(None, "mp"),
            P(None, DP, None),
            P(None, DP, None),
        ),
        out_specs=(
            P(both, None),
            P(both, None, "mp"),
            P(None, both, None, "mp"),
            P("mp", None),
            P(None, "mp"),
        ),
        check_vma=False,
    )
```

```python
import jax
import jax.numpy as jnp
import numpy as np
from jax import lax
from jax.experimental import pallas as pl
from jax.experimental.pallas import tpu as pltpu
from jax.sharding import Mesh, PartitionSpec as P

HEAD = 128
KL = 0.1
DECAY = 0.95
EPS = 1e-05
MASKED = -1e30
SMALL = 2.0 ** -20
F32 = jnp.float32
BF16 = jnp.bfloat16
NT = (((1,), (1,)), ((), ()))
NN = (((1,), (0,)), ((), ()))
TN = (((0,), (0,)), ((), ()))


def dot(a, b, dims):
    return lax.dot_general(a, b, dims, preferred_element_type=F32)


def halves(x):
    high = x.astype(BF16)
    return high, (x - high.astype(F32)).astype(BF16)


def as_column(row):
    n = row.shape[1]
    return jnp.broadcast_to(row, (n, n)).T


def square(row):
    n = row.shape[1]
    return jnp.broadcast_to(row, (n, n))


def kept_of(doc_row, groups):
    n = doc_row.shape[1]
    doc = doc_row.astype(F32)
    rows = lax.broadcasted_iota(jnp.int32, (n, n), 0)
    lanes = lax.broadcasted_iota(jnp.int32, (n, n), 1)
    kept = jnp.where((as_column(doc) == square(doc)) & (rows <= lanes), 1.0, 0.0)
    return jnp.concatenate([kept] * groups, axis=1) > 0.5


def stacked(ref, group, groups):
    first = group * groups
    return jnp.concatenate([ref[:, (first + i) * HEAD:(first + i + 1) * HEAD] for i in range(groups)], axis=0)


def probs_of(query, keys, kept):
    scores = dot(keys, query, NT)
    scores = jnp.where(kept, scores, MASKED)
    top = jnp.max(scores, axis=0, keepdims=True)
    raised = jnp.exp((scores - top) * HEAD ** (-0.5))
    return raised * (1.0 / jnp.sum(raised, axis=0, keepdims=True))


def scorer_kernel(doc_ref, q_ref, k_ref, v_ref, after_ref, out_ref):
    del after_ref
    n = q_ref.shape[0]
    groups = q_ref.shape[1] // k_ref.shape[1]
    kept = kept_of(doc_ref[...], groups)
    for group in range(k_ref.shape[1] // HEAD):
        kv = slice(group * HEAD, (group + 1) * HEAD)
        probs = probs_of(stacked(q_ref, group, groups), k_ref[:, kv], kept).astype(BF16)
        attended = dot(probs, v_ref[:, kv], TN)
        for i in range(groups):
            at = (group * groups + i) * HEAD
            out_ref[:, at:at + HEAD] = attended[i * n:(i + 1) * n]


def score_kernel(sec_ref, att_ref, own_ref, next_ref, after_ref, last_ref, heads_ref, out_ref):
    sec = sec_ref[0]
    n_sec = att_ref.shape[0]
    copies = out_ref.shape[0] // n_sec
    n_heads = att_ref.shape[2] // HEAD
    held = (own_ref, next_ref, after_ref, last_ref)

    def put(weight):
        for step in range(n_sec):
            row = lax.rem(sec + step, n_sec)
            total = None
            for head in range(n_heads):
                at = slice(head * HEAD, (head + 1) * HEAD)
                term = att_ref[row, :, at] * weight(step, at)
                total = term if total is None else total + term
            score = jnp.sum(total.T, axis=0, keepdims=True)
            for copy in range(copies):
                out_ref[row * copies + copy] = score

    @pl.when(sec < 2)
    def _():
        put(lambda step, at: held[step][:, at].astype(F32))

    @pl.when(sec >= 2)
    def _():
        put(lambda step, at: jnp.where(sec == 2, heads_ref[0:1, at], heads_ref[1:2, at]))


def policy_kernel(sec_ref, doc_ref, q_ref, memory_ref, rows_ref, adapter_ref, down_ref, up_ref,
                  att_ref, probs_ref, part_ref):
    k_ref, v_ref = memory_ref.at[0, 0], memory_ref.at[1, 0]
    n = q_ref.shape[0]
    groups = q_ref.shape[1] // k_ref.shape[1]
    kept = kept_of(doc_ref[sec_ref[0]], groups)
    base = None
    low_in = None
    for group in range(k_ref.shape[1] // HEAD):
        kv = slice(group * HEAD, (group + 1) * HEAD)
        probs = probs_of(stacked(q_ref, group, groups), k_ref[:, kv], kept)
        probs_ref[group] = probs
        attended = dot(probs.astype(BF16), v_ref[:, kv], TN)
        for i in range(groups):
            at = slice((group * groups + i) * HEAD, (group * groups + i + 1) * HEAD)
            own = attended[i * n:(i + 1) * n]
            att_ref[:, at] = own
            term = own * rows_ref[:, at].astype(F32)
            base = term if base is None else base + term
            high, low = halves(own)
            down = down_ref[:, at]
            term = dot(down, high, NT) + dot(down, low, NT)
            low_in = term if low_in is None else low_in + term
    rank = down_ref.shape[0]
    part_ref[0:rank, :] = low_in
    part_ref[rank:2 * rank, :] = dot(up_ref[...], adapter_ref[...], NT)
    base_row = jnp.sum(base.T, axis=0, keepdims=True)
    part_ref[2 * rank:, :] = jnp.broadcast_to(base_row, (8, base_row.shape[1]))


def pick(row, index):
    lane = lax.broadcasted_iota(jnp.int32, row.shape, 1)
    return jnp.sum(jnp.where(lane == index, row, 0.0), axis=1, keepdims=True)


def weights_kernel(sec_ref, core_ref, prompt_ref, doc_ref, got_ref, att_ref, adapter_ref,
                   part0, part1, part2, part3,
                   keep_ref, low_ref, own_ref, send_ref, both_ref):
    sec = sec_ref[0]
    doc = doc_ref[sec].astype(F32)
    n = doc.shape[1]
    doc_col, doc_row = as_column(doc), square(doc)
    rows = lax.broadcasted_iota(jnp.int32, (n, n), 0)
    lanes = lax.broadcasted_iota(jnp.int32, (n, n), 1)
    position = lax.broadcasted_iota(jnp.int32, (1, n), 1).astype(F32)
    start = jnp.sum(jnp.where(doc_col < doc_row, 1.0, 0.0), axis=0, keepdims=True)
    ending = jnp.sum(jnp.where(doc_col <= doc_row, 1.0, 0.0), axis=0, keepdims=True) - 1.0
    prompt = jnp.zeros((1, n), F32)
    for label in range(prompt_ref.shape[1]):
        length = prompt_ref[sec, label].astype(F32)
        prompt = jnp.where(doc == float(label), length, prompt)
    respond = jnp.where(position - start >= prompt, 1.0, 0.0)
    closing = jnp.where(position == ending, 1.0, 0.0)

    def section(index):
        return jnp.sum(got_ref[index], axis=0, keepdims=True)

    old, ref, reward, value = section(0), section(1), section(2), section(3)
    next_value = jnp.where(position < n - 1.0, pltpu.roll(value, n - 1, 1), 0.0) * (1.0 - closing)
    delta = -KL * (old - ref) + closing * reward + next_value - value
    later = rows - lanes
    linked = (doc_col == doc_row) & (later >= 0)
    powers = jnp.exp(jnp.maximum(later, 0).astype(F32) * float(np.log(DECAY)))
    terms = jnp.where(linked, powers, 0.0) * as_column(delta)
    advantage = jnp.sum(terms, axis=0, keepdims=True)
    lane = lax.broadcasted_iota(jnp.int32, (1, n), 1)
    count = jnp.sum(respond, axis=1, keepdims=True)
    total = jnp.sum(respond * advantage, axis=1, keepdims=True)
    squares = jnp.sum(respond * advantage * advantage, axis=1, keepdims=True)
    moments = jnp.where(lane == 0, count, jnp.where(lane == 1, total, jnp.where(lane == 2, squares, 0.0)))

    rank = (part0.shape[0] - 8) // 2
    part = (part0[...] + part1[...]) + (part2[...] + part3[...])
    low_in, low_out, base = part[0:rank], part[rank:2 * rank], part[2 * rank:2 * rank + 1]
    policy_new = base + jnp.sum(low_in * low_out, axis=0, keepdims=True)
    weight = -respond * jnp.exp(policy_new - old)
    keep_ref[0:1, :] = respond
    keep_ref[1:2, :] = advantage
    keep_ref[2:3, :] = weight
    keep_ref[3:8, :] = jnp.zeros((5, n), F32)
    low_ref[...] = low_out
    plain = weight * SMALL
    lifted = plain * advantage
    out_high, out_low = halves(jnp.concatenate([plain * low_out, lifted * low_out], axis=0))
    in_high, in_low = halves(jnp.concatenate([plain * low_in, lifted * low_in], axis=0))
    n_down = att_ref.shape[1] // HEAD
    cores = both_ref.shape[0]
    slots = (n_down + adapter_ref.shape[1] // HEAD) // cores
    half = slots * rank
    for block in range(cores * slots):
        if block < n_down:
            high, low = halves(att_ref[:, block * HEAD:(block + 1) * HEAD])
            term = dot(out_high, high, NN) + (dot(out_low, high, NN) + dot(out_high, low, NN))
        else:
            at = (block - n_down) * HEAD
            columns = adapter_ref[:, at:at + HEAD]
            term = dot(in_high, columns, NN) + dot(in_low, columns, NN)
        owner, at = block // slots, block % slots * rank
        both_ref[owner, at:at + rank] = term[0:rank]
        both_ref[owner, half + at:half + at + rank] = term[rank:]
    for owner in range(cores):
        both_ref[owner, 2 * half:] = jnp.broadcast_to(moments, (8, n))
    core = core_ref[0]
    own_ref[...] = both_ref[core]
    send_ref[...] = both_ref[cores - 1 - core]


def middle(moments):
    near = pick(moments, 1) / jnp.maximum(pick(moments, 0), 1.0)
    return near.astype(BF16).astype(F32)


def note(moments, centre):
    n = moments.shape[1]
    first = moments.astype(BF16).astype(F32)
    rest = moments - first
    second = rest.astype(BF16).astype(F32)
    third = rest - second
    lane = lax.broadcasted_iota(jnp.int32, moments.shape, 1)
    first = jnp.where(lane == 3, centre, first)
    row = lax.broadcasted_iota(jnp.int32, (16, n), 0)
    return jnp.where(row == 0, first, jnp.where(row == 1, second, jnp.where(row == 2, third, 0.0))).astype(BF16)


def pair_kernel(own_ref, got_ref, out_ref):
    n_z, per = out_ref.shape[0], (out_ref.shape[1] - 16) // 2
    half = n_z * per
    moments = own_ref[2 * half:2 * half + 1] + got_ref[2 * half:2 * half + 1]
    centre = middle(moments)
    tile = note(moments, centre)
    for slot in range(n_z):
        at = slice(slot * per, (slot + 1) * per)
        to = slice(half + slot * per, half + (slot + 1) * per)
        plain = own_ref[at] + got_ref[at]
        lifted = own_ref[to] + got_ref[to]
        out_ref[slot, 0:per] = plain.astype(BF16)
        out_ref[slot, per:2 * per] = (lifted - centre * plain).astype(BF16)
        out_ref[slot, 2 * per:] = tile


def gathered(got_ref, per):
    notes = [jnp.sum(got_ref[i, 2 * per:].astype(F32), axis=0, keepdims=True) for i in range(got_ref.shape[0])]
    lane = lax.broadcasted_iota(jnp.int32, notes[0].shape, 1)
    moments = notes[0]
    for other in notes[1:]:
        moments = moments + other
    return jnp.where(lane < 3, moments, 0.0), [pick(x, 3) for x in notes]


def added(got_ref, per, centres, centre):
    plain, lifted = None, None
    for index in range(got_ref.shape[0]):
        mine = got_ref[index, 0:per].astype(F32)
        high = got_ref[index, per:2 * per].astype(F32) + (centres[index] - centre) * mine
        plain = mine if plain is None else plain + mine
        lifted = high if lifted is None else lifted + high
    return plain, lifted


def column_kernel(got_ref, out_ref):
    per = (got_ref.shape[1] - 16) // 2
    moments, centres = gathered(got_ref, per)
    centre = middle(moments)
    plain, lifted = added(got_ref, per, centres, centre)
    plain, lifted = plain.astype(BF16), lifted.astype(BF16)
    tile = note(moments, centre)
    for index in range(out_ref.shape[0]):
        out_ref[index, 0:per] = plain
        out_ref[index, per:2 * per] = lifted
        out_ref[index, 2 * per:] = tile


def scale_of(moments):
    count = pick(moments, 0)
    mean = pick(moments, 1) / count
    spread = pick(moments, 2) / count - mean * mean
    return count, mean, lax.rsqrt(spread + EPS)


def final_kernel(got_ref, out_ref, moments_ref):
    per = (got_ref.shape[1] - 16) // 2
    moments, centres = gathered(got_ref, per)
    count, mean, scale = scale_of(moments)
    _, lifted = added(got_ref, per, centres, mean)
    total = (lifted * (scale / count * (1.0 / SMALL))).astype(BF16)
    for index in range(out_ref.shape[0]):
        out_ref[index] = total
    moments_ref[...] = jnp.broadcast_to(moments, moments_ref.shape)


def place_kernel(core_ref, own_ref, other_ref, down_ref, up_ref, both_ref):
    core = core_ref[0]
    slots = own_ref.shape[0]
    cores = both_ref.shape[0] // slots
    for slot in range(slots):
        both_ref[(cores - 1 - core) * slots + slot] = other_ref[slot]
        both_ref[core * slots + slot] = own_ref[slot]
    n_down = down_ref.shape[1] // HEAD
    for block in range(both_ref.shape[0]):
        value = both_ref[block].astype(F32)
        if block < n_down:
            down_ref[:, block * HEAD:(block + 1) * HEAD] = value
        else:
            at = (block - n_down) * HEAD
            up_ref[:, at:at + HEAD] = value


def backward_kernel(moments_ref, keep_ref, low_ref, down_ref, rows_ref, probs_ref, q_ref, memory_ref,
                    white_ref, query_ref, memory_grad_ref):
    k_ref, v_ref = memory_ref.at[0, 0], memory_ref.at[1, 0]
    n = q_ref.shape[0]
    count, mean, inverse = scale_of(moments_ref[0:1, :])
    whitened = keep_ref[0:1, :] * (keep_ref[1:2, :] - mean) * inverse
    white_ref[...] = whitened
    grad_score = keep_ref[2:3, :] * whitened / count
    grad_col = as_column(grad_score)
    high, low = halves(grad_score * low_ref[...])
    groups = q_ref.shape[1] // k_ref.shape[1]
    scale = HEAD ** (-0.5)
    for group in range(k_ref.shape[1] // HEAD):
        kv = slice(group * HEAD, (group + 1) * HEAD)
        keys, values = k_ref[:, kv], v_ref[:, kv]
        grads = []
        for head in range(group * groups, (group + 1) * groups):
            at = slice(head * HEAD, (head + 1) * HEAD)
            down = down_ref[:, at]
            grad = grad_col * rows_ref[:, at].astype(F32) + (dot(high, down, TN) + dot(low, down, TN))
            grads.append(grad.astype(BF16))
        grad = jnp.concatenate(grads, axis=0)
        probs = probs_ref[group]
        dprobs = dot(values, grad, NT)
        inner = jnp.sum(probs * dprobs, axis=0, keepdims=True)
        dscores = (probs * (dprobs - inner)).astype(BF16)
        query_grad = (dot(dscores, keys, TN) * scale).astype(BF16)
        for i in range(groups):
            at = (group * groups + i) * HEAD
            query_ref[:, at:at + HEAD] = query_grad[i * n:(i + 1) * n]
        memory_grad_ref[0, 0, :, kv] = (dot(dscores, stacked(q_ref, group, groups), NN) * scale).astype(BF16)
        memory_grad_ref[1, 0, :, kv] = dot(probs.astype(BF16), grad, NN).astype(BF16)


def call(kernel, outs, args, smem=(), scratch=(), **params):
    specs = [pl.BlockSpec(memory_space=pltpu.SMEM if i in smem else pltpu.VMEM) for i in range(len(args))]
    return pl.pallas_call(
        kernel,
        out_shape=outs,
        in_specs=specs,
        out_specs=jax.tree.map(lambda _: pl.BlockSpec(memory_space=pltpu.VMEM), outs),
        scratch_shapes=scratch,
        compiler_params=pltpu.CompilerParams(vmem_limit_bytes=16 * 2**20),
        interpret=INTERPRET,
        **params,
    )(*args)


def sds(shape, dtype=F32):
    return jax.ShapeDtypeStruct(shape, dtype)


INTERPRET = False
SPLIT = (2, 12, 2)
AXES = ("sec", "yh", "z", "core", "mp")
DP = ("yh", "z", "core")
Y = ("sec", "yh")


def exchange(x, axes):
    return lax.all_to_all(x, axes, 0, 0, tiled=True)


def swap(x, n):
    return lax.ppermute(x, "core", [(i, n - 1 - i) for i in range(n)])


def on_device(policy_query, policy_memory, chosen, adapter_rows, adapter_down, adapter_up,
              scorer_query, scorer_key_values, score_heads, document_ids, prompt_lengths):
    sec = lax.axis_index("sec").astype(jnp.int32).reshape(1)
    core = lax.axis_index("core").astype(jnp.int32).reshape(1)
    n_sec, n_mp = lax.axis_size("sec"), lax.axis_size("mp")
    n_yh, n_z, n_core = (lax.axis_size(a) for a in DP)
    n_y = n_sec * n_yh
    query = policy_query[0]
    rows = chosen[0]
    tokens, features = query.shape
    kv_features = policy_memory.shape[3]
    adapter = adapter_rows[0]
    down = adapter_down.T
    rank = down.shape[0]
    width = adapter.shape[1]
    heads = features // HEAD
    prompts = prompt_lengths[:, 0]
    blocks = (features + width) // HEAD
    half = blocks // n_core * rank
    per = half // n_z

    held = (
        rows,
        lax.ppermute(rows, "sec", [(1, 0), (2, 1)]),
        lax.ppermute(rows, "sec", [(2, 0), (3, 1)]),
        lax.ppermute(rows, "sec", [(3, 0), (0, 1)]),
    )
    attended, probs, part = call(
        policy_kernel,
        (sds((tokens, features)), sds((kv_features // HEAD, tokens, heads * HEAD * tokens // kv_features)), sds((2 * rank + 8, tokens))),
        (sec, document_ids, query, policy_memory, rows, adapter, down, adapter_up),
        smem=(0,),
        cost_estimate=pl.CostEstimate(flops=150_000_000, bytes_accessed=3_000_000, transcendentals=150_000),
    )
    parts = (part,) + tuple(
        lax.ppermute(part, "mp", [(i, (i + k) % n_mp) for i in range(n_mp)]) for k in range(1, n_mp)
    )
    scorer = pl.pallas_call(
        scorer_kernel,
        grid=(n_sec,),
        out_shape=sds((n_sec, tokens, features)),
        in_specs=[
            pl.BlockSpec((None, 1, tokens), lambda j: (j, 0, 0)),
            pl.BlockSpec((None, None, None, tokens, features), lambda j: (0, j, 0, 0, 0)),
            pl.BlockSpec((None, None, None, None, tokens, kv_features), lambda j: (0, 0, j, 0, 0, 0)),
            pl.BlockSpec((None, None, None, None, tokens, kv_features), lambda j: (0, 1, j, 0, 0, 0)),
            pl.BlockSpec(memory_space=pl.ANY),
        ],
        out_specs=pl.BlockSpec((None, tokens, features), lambda j: (j, 0, 0)),
        compiler_params=pltpu.CompilerParams(vmem_limit_bytes=16 * 2**20),
        interpret=INTERPRET,
        cost_estimate=pl.CostEstimate(flops=300_000_000, bytes_accessed=30_000_000, transcendentals=600_000),
    )
    scorer_att = scorer(document_ids, scorer_query, scorer_key_values, scorer_key_values, part)
    partials = call(score_kernel, sds((n_sec * n_mp, 1, tokens)), (sec, scorer_att) + held + (score_heads,),
                    smem=(0,),
                    cost_estimate=pl.CostEstimate(flops=2_000_000, bytes_accessed=3_000_000, transcendentals=0))
    got = exchange(partials, ("sec", "mp")).reshape(n_sec, n_mp, tokens)
    keep, low_out, own, send = call(
        weights_kernel,
        (sds((8, tokens)), sds((rank, tokens)), sds((2 * half + 8, HEAD)), sds((2 * half + 8, HEAD))),
        (sec, core, prompts, document_ids, got, attended, adapter) + parts,
        smem=(0, 1, 2),
        scratch=(pltpu.VMEM((n_core, 2 * half + 8, HEAD), F32),),
    )
    got = call(pair_kernel, sds((n_z, 2 * per + 16, HEAD), BF16), (own, swap(send, n_core)))
    got = exchange(got, "z")
    got = exchange(call(column_kernel, sds((n_y, 2 * per + 16, HEAD), BF16), (got,)), Y)
    got, moments = call(final_kernel, (sds((n_z, per, HEAD), BF16), sds((8, HEAD))), (got,))
    got = exchange(got, "z")
    got = got.reshape(blocks // n_core, rank, HEAD)
    down_grad, up_grad = call(place_kernel, (sds((rank, features)), sds((rank, width))),
                              (core, got, swap(got, n_core)), smem=(0,),
                              scratch=(pltpu.VMEM((blocks, rank, HEAD), BF16),))
    white, query_grad, memory_grad = call(
        backward_kernel,
        (sds((1, tokens)), sds((tokens, features), BF16), sds(policy_memory.shape, BF16)),
        (moments, keep, low_out, down, rows, probs, query, policy_memory),
        cost_estimate=pl.CostEstimate(flops=300_000_000, bytes_accessed=20_000_000, transcendentals=0),
    )
    return white, query_grad[None], memory_grad, down_grad.T, up_grad


def solution(mesh):
    devices = mesh.devices
    split = SPLIT if int(np.prod(SPLIT)) == devices.shape[1] else (1, devices.shape[1], 1)
    inner = Mesh(devices.reshape((devices.shape[0],) + split + (devices.shape[2],)), AXES)
    both = ("sec",) + DP

    return jax.shard_map(
        on_device,
        mesh=inner,
        in_specs=(
            P(both, None, "mp"),
            P(None, both, None, "mp"),
            P(both, None, "mp"),
            P(both, None, "mp"),
            P("mp", None),
            P(None, "mp"),
            P("sec", None, DP, None, "mp"),
            P("sec", None, None, DP, None, "mp"),
            P(None, "mp"),
            P(None, DP, None),
            P(None, DP, None),
        ),
        out_specs=(
            P(both, None),
            P(both, None, "mp"),
            P(None, both, None, "mp"),
            P("mp", None),
            P(None, "mp"),
        ),
        check_vma=False,
    )
```

```python
import jax
import jax.numpy as jnp
import numpy as np
from jax import lax
from jax.experimental import pallas as pl
from jax.experimental.pallas import tpu as pltpu
from jax.sharding import Mesh, PartitionSpec as P

HEAD = 128
KL = 0.1
DECAY = 0.95
EPS = 1e-05
MASKED = -1e30
SMALL = 2.0 ** -20
F32 = jnp.float32
BF16 = jnp.bfloat16
NT = (((1,), (1,)), ((), ()))
NN = (((1,), (0,)), ((), ()))
TN = (((0,), (0,)), ((), ()))


def dot(a, b, dims):
    return lax.dot_general(a, b, dims, preferred_element_type=F32)


def halves(x):
    high = x.astype(BF16)
    return high, (x - high.astype(F32)).astype(BF16)


def as_column(row):
    n = row.shape[1]
    return jnp.broadcast_to(row, (n, n)).T


def square(row):
    n = row.shape[1]
    return jnp.broadcast_to(row, (n, n))


def kept_of(doc_row, groups):
    n = doc_row.shape[1]
    doc = doc_row.astype(F32)
    rows = lax.broadcasted_iota(jnp.int32, (n, n), 0)
    lanes = lax.broadcasted_iota(jnp.int32, (n, n), 1)
    kept = jnp.where((as_column(doc) == square(doc)) & (rows <= lanes), 1.0, 0.0)
    return jnp.concatenate([kept] * groups, axis=1) > 0.5


def stacked(ref, group, groups):
    first = group * groups
    return jnp.concatenate([ref[:, (first + i) * HEAD:(first + i + 1) * HEAD] for i in range(groups)], axis=0)


def probs_of(query, keys, kept):
    scores = dot(keys, query, NT)
    scores = jnp.where(kept, scores, MASKED)
    top = jnp.max(scores, axis=0, keepdims=True)
    raised = jnp.exp((scores - top) * HEAD ** (-0.5))
    return raised * (1.0 / jnp.sum(raised, axis=0, keepdims=True))


def scorer_kernel(doc_ref, q_ref, k_ref, v_ref, out_ref, last_ref):
    n = q_ref.shape[0]
    groups = q_ref.shape[1] // k_ref.shape[1]
    kept = kept_of(doc_ref[...], groups)
    for group in range(k_ref.shape[1] // HEAD):
        kv = slice(group * HEAD, (group + 1) * HEAD)
        probs = probs_of(stacked(q_ref, group, groups), k_ref[:, kv], kept).astype(BF16)
        attended = dot(probs, v_ref[:, kv], TN)
        for i in range(groups):
            at = (group * groups + i) * HEAD
            out_ref[:, at:at + HEAD] = attended[i * n:(i + 1) * n]

    @pl.when(pl.program_id(0) == pl.num_programs(0) - 1)
    def _():
        last_ref[...] = out_ref[...].astype(BF16)


def score_kernel(sec_ref, att_ref, own_ref, next_ref, other_ref, first_ref, second_ref, heads_ref, out_ref):
    sec = sec_ref[0]
    n_sec = att_ref.shape[0]
    copies = out_ref.shape[0] // n_sec
    n_heads = att_ref.shape[2] // HEAD
    late = n_sec - 1

    def score(left, right):
        total = None
        for head in range(n_heads):
            at = slice(head * HEAD, (head + 1) * HEAD)
            term = left(at) * right(at)
            total = term if total is None else total + term
        return jnp.sum(total.T, axis=0, keepdims=True)

    def put(row, index, value):
        for copy in range(copies):
            out_ref[row * copies + copy, index:index + 1] = value

    out_ref[...] = jnp.zeros(out_ref.shape, F32)

    @pl.when(sec < 2)
    def _():
        for held, row in ((own_ref, sec), (next_ref, sec + 1), (other_ref, 2 - 2 * sec)):
            put(row, 0, score(lambda at: att_ref[row, :, at], lambda at: held[:, at].astype(F32)))

    @pl.when(sec >= 2)
    def _():
        def weight(at):
            return jnp.where(sec == 2, heads_ref[0:1, at], heads_ref[1:2, at])

        for row in range(n_sec):
            put(row, 0, score(lambda at: att_ref[row, :, at], weight))

    @pl.when(sec == late)
    def _():
        for index, held in ((1, first_ref), (2, second_ref)):
            put(late, index, score(lambda at: held[:, at].astype(F32), lambda at: own_ref[:, at].astype(F32)))


def policy_kernel(sec_ref, doc_ref, q_ref, memory_ref, rows_ref, adapter_ref, down_ref, up_ref, after_ref,
                  att_ref, probs_ref, part_ref):
    del after_ref
    k_ref, v_ref = memory_ref.at[0, 0], memory_ref.at[1, 0]
    n = q_ref.shape[0]
    groups = q_ref.shape[1] // k_ref.shape[1]
    kept = kept_of(doc_ref[sec_ref[0]], groups)
    base = None
    low_in = None
    for group in range(k_ref.shape[1] // HEAD):
        kv = slice(group * HEAD, (group + 1) * HEAD)
        probs = probs_of(stacked(q_ref, group, groups), k_ref[:, kv], kept)
        probs_ref[group] = probs
        attended = dot(probs.astype(BF16), v_ref[:, kv], TN)
        for i in range(groups):
            at = slice((group * groups + i) * HEAD, (group * groups + i + 1) * HEAD)
            own = attended[i * n:(i + 1) * n]
            att_ref[:, at] = own
            term = own * rows_ref[:, at].astype(F32)
            base = term if base is None else base + term
            high, low = halves(own)
            down = down_ref[:, at]
            term = dot(down, high, NT) + dot(down, low, NT)
            low_in = term if low_in is None else low_in + term
    rank = down_ref.shape[0]
    part_ref[0:rank, :] = low_in
    part_ref[rank:2 * rank, :] = dot(up_ref[...], adapter_ref[...], NT)
    base_row = jnp.sum(base.T, axis=0, keepdims=True)
    part_ref[2 * rank:, :] = jnp.broadcast_to(base_row, (8, base_row.shape[1]))


def pick(row, index):
    lane = lax.broadcasted_iota(jnp.int32, row.shape, 1)
    return jnp.sum(jnp.where(lane == index, row, 0.0), axis=1, keepdims=True)


def weights_kernel(sec_ref, core_ref, prompt_ref, doc_ref, got_ref, att_ref, adapter_ref,
                   part0, part1, part2, part3,
                   keep_ref, low_ref, own_ref, send_ref, both_ref):
    sec = sec_ref[0]
    doc = doc_ref[sec].astype(F32)
    n = doc.shape[1]
    doc_col, doc_row = as_column(doc), square(doc)
    rows = lax.broadcasted_iota(jnp.int32, (n, n), 0)
    lanes = lax.broadcasted_iota(jnp.int32, (n, n), 1)
    position = lax.broadcasted_iota(jnp.int32, (1, n), 1).astype(F32)
    start = jnp.sum(jnp.where(doc_col < doc_row, 1.0, 0.0), axis=0, keepdims=True)
    ending = jnp.sum(jnp.where(doc_col <= doc_row, 1.0, 0.0), axis=0, keepdims=True) - 1.0
    prompt = jnp.zeros((1, n), F32)
    for label in range(prompt_ref.shape[1]):
        length = prompt_ref[sec, label].astype(F32)
        prompt = jnp.where(doc == float(label), length, prompt)
    respond = jnp.where(position - start >= prompt, 1.0, 0.0)
    closing = jnp.where(position == ending, 1.0, 0.0)

    def section(index):
        total = jnp.sum(got_ref[index, :, 0, :], axis=0, keepdims=True)
        if index < 2:
            total = total + jnp.sum(got_ref[3, :, index + 1, :], axis=0, keepdims=True)
        return total

    old, ref, reward, value = section(0), section(1), section(2), section(3)
    next_value = jnp.where(position < n - 1.0, pltpu.roll(value, n - 1, 1), 0.0) * (1.0 - closing)
    delta = -KL * (old - ref) + closing * reward + next_value - value
    later = rows - lanes
    linked = (doc_col == doc_row) & (later >= 0)
    powers = jnp.exp(jnp.maximum(later, 0).astype(F32) * float(np.log(DECAY)))
    terms = jnp.where(linked, powers, 0.0) * as_column(delta)
    advantage = jnp.sum(terms, axis=0, keepdims=True)
    lane = lax.broadcasted_iota(jnp.int32, (1, n), 1)
    count = jnp.sum(respond, axis=1, keepdims=True)
    total = jnp.sum(respond * advantage, axis=1, keepdims=True)
    squares = jnp.sum(respond * advantage * advantage, axis=1, keepdims=True)
    moments = jnp.where(lane == 0, count, jnp.where(lane == 1, total, jnp.where(lane == 2, squares, 0.0)))

    rank = (part0.shape[0] - 8) // 2
    part = (part0[...] + part1[...]) + (part2[...] + part3[...])
    low_in, low_out, base = part[0:rank], part[rank:2 * rank], part[2 * rank:2 * rank + 1]
    policy_new = base + jnp.sum(low_in * low_out, axis=0, keepdims=True)
    weight = -respond * jnp.exp(policy_new - old)
    keep_ref[0:1, :] = respond
    keep_ref[1:2, :] = advantage
    keep_ref[2:3, :] = weight
    keep_ref[3:8, :] = jnp.zeros((5, n), F32)
    low_ref[...] = low_out
    plain = weight * SMALL
    lifted = plain * advantage
    out_high, out_low = halves(jnp.concatenate([plain * low_out, lifted * low_out], axis=0))
    in_high, in_low = halves(jnp.concatenate([plain * low_in, lifted * low_in], axis=0))
    n_down = att_ref.shape[1] // HEAD
    cores = both_ref.shape[0]
    slots = (n_down + adapter_ref.shape[1] // HEAD) // cores
    half = slots * rank
    for block in range(cores * slots):
        if block < n_down:
            high, low = halves(att_ref[:, block * HEAD:(block + 1) * HEAD])
            term = dot(out_high, high, NN) + (dot(out_low, high, NN) + dot(out_high, low, NN))
        else:
            at = (block - n_down) * HEAD
            columns = adapter_ref[:, at:at + HEAD]
            term = dot(in_high, columns, NN) + dot(in_low, columns, NN)
        owner, at = block // slots, block % slots * rank
        both_ref[owner, at:at + rank] = term[0:rank]
        both_ref[owner, half + at:half + at + rank] = term[rank:]
    for owner in range(cores):
        both_ref[owner, 2 * half:] = jnp.broadcast_to(moments, (8, n))
    core = core_ref[0]
    own_ref[...] = both_ref[core]
    send_ref[...] = both_ref[cores - 1 - core]


def middle(moments):
    near = pick(moments, 1) / jnp.maximum(pick(moments, 0), 1.0)
    return near.astype(BF16).astype(F32)


def note(moments, centre):
    n = moments.shape[1]
    first = moments.astype(BF16).astype(F32)
    rest = moments - first
    second = rest.astype(BF16).astype(F32)
    third = rest - second
    lane = lax.broadcasted_iota(jnp.int32, moments.shape, 1)
    first = jnp.where(lane == 3, centre, first)
    row = lax.broadcasted_iota(jnp.int32, (16, n), 0)
    return jnp.where(row == 0, first, jnp.where(row == 1, second, jnp.where(row == 2, third, 0.0))).astype(BF16)


def pair_kernel(own_ref, got_ref, out_ref):
    n_z, per = out_ref.shape[0], (out_ref.shape[1] - 16) // 2
    half = n_z * per
    moments = own_ref[2 * half:2 * half + 1] + got_ref[2 * half:2 * half + 1]
    centre = middle(moments)
    tile = note(moments, centre)
    for slot in range(n_z):
        at = slice(slot * per, (slot + 1) * per)
        to = slice(half + slot * per, half + (slot + 1) * per)
        plain = own_ref[at] + got_ref[at]
        lifted = own_ref[to] + got_ref[to]
        out_ref[slot, 0:per] = plain.astype(BF16)
        out_ref[slot, per:2 * per] = (lifted - centre * plain).astype(BF16)
        out_ref[slot, 2 * per:] = tile


def gathered(got_ref, per):
    notes = [jnp.sum(got_ref[i, 2 * per:].astype(F32), axis=0, keepdims=True) for i in range(got_ref.shape[0])]
    lane = lax.broadcasted_iota(jnp.int32, notes[0].shape, 1)
    moments = notes[0]
    for other in notes[1:]:
        moments = moments + other
    return jnp.where(lane < 3, moments, 0.0), [pick(x, 3) for x in notes]


def added(got_ref, per, centres, centre):
    plain, lifted = None, None
    for index in range(got_ref.shape[0]):
        mine = got_ref[index, 0:per].astype(F32)
        high = got_ref[index, per:2 * per].astype(F32) + (centres[index] - centre) * mine
        plain = mine if plain is None else plain + mine
        lifted = high if lifted is None else lifted + high
    return plain, lifted


def column_kernel(got_ref, out_ref):
    per = (got_ref.shape[1] - 16) // 2
    moments, centres = gathered(got_ref, per)
    centre = middle(moments)
    plain, lifted = added(got_ref, per, centres, centre)
    plain, lifted = plain.astype(BF16), lifted.astype(BF16)
    tile = note(moments, centre)
    for index in range(out_ref.shape[0]):
        out_ref[index, 0:per] = plain
        out_ref[index, per:2 * per] = lifted
        out_ref[index, 2 * per:] = tile


def scale_of(moments):
    count = pick(moments, 0)
    mean = pick(moments, 1) / count
    spread = pick(moments, 2) / count - mean * mean
    return count, mean, lax.rsqrt(spread + EPS)


def final_kernel(got_ref, out_ref, moments_ref):
    per = (got_ref.shape[1] - 16) // 2
    moments, centres = gathered(got_ref, per)
    count, mean, scale = scale_of(moments)
    _, lifted = added(got_ref, per, centres, mean)
    total = (lifted * (scale / count * (1.0 / SMALL))).astype(BF16)
    for index in range(out_ref.shape[0]):
        out_ref[index] = total
    moments_ref[...] = jnp.broadcast_to(moments, moments_ref.shape)


def place_kernel(core_ref, own_ref, other_ref, down_ref, up_ref, both_ref):
    core = core_ref[0]
    slots = own_ref.shape[0]
    cores = both_ref.shape[0] // slots
    for slot in range(slots):
        both_ref[(cores - 1 - core) * slots + slot] = other_ref[slot]
        both_ref[core * slots + slot] = own_ref[slot]
    n_down = down_ref.shape[1] // HEAD
    for block in range(both_ref.shape[0]):
        value = both_ref[block].astype(F32)
        if block < n_down:
            down_ref[:, block * HEAD:(block + 1) * HEAD] = value
        else:
            at = (block - n_down) * HEAD
            up_ref[:, at:at + HEAD] = value


def backward_kernel(moments_ref, keep_ref, low_ref, down_ref, rows_ref, probs_ref, q_ref, memory_ref,
                    white_ref, query_ref, memory_grad_ref):
    k_ref, v_ref = memory_ref.at[0, 0], memory_ref.at[1, 0]
    n = q_ref.shape[0]
    count, mean, inverse = scale_of(moments_ref[0:1, :])
    whitened = keep_ref[0:1, :] * (keep_ref[1:2, :] - mean) * inverse
    white_ref[...] = whitened
    grad_score = keep_ref[2:3, :] * whitened / count
    grad_col = as_column(grad_score)
    high, low = halves(grad_score * low_ref[...])
    groups = q_ref.shape[1] // k_ref.shape[1]
    scale = HEAD ** (-0.5)
    for group in range(k_ref.shape[1] // HEAD):
        kv = slice(group * HEAD, (group + 1) * HEAD)
        keys, values = k_ref[:, kv], v_ref[:, kv]
        grads = []
        for head in range(group * groups, (group + 1) * groups):
            at = slice(head * HEAD, (head + 1) * HEAD)
            down = down_ref[:, at]
            grad = grad_col * rows_ref[:, at].astype(F32) + (dot(high, down, TN) + dot(low, down, TN))
            grads.append(grad.astype(BF16))
        grad = jnp.concatenate(grads, axis=0)
        probs = probs_ref[group]
        dprobs = dot(values, grad, NT)
        inner = jnp.sum(probs * dprobs, axis=0, keepdims=True)
        dscores = (probs * (dprobs - inner)).astype(BF16)
        query_grad = (dot(dscores, keys, TN) * scale).astype(BF16)
        for i in range(groups):
            at = (group * groups + i) * HEAD
            query_ref[:, at:at + HEAD] = query_grad[i * n:(i + 1) * n]
        memory_grad_ref[0, 0, :, kv] = (dot(dscores, stacked(q_ref, group, groups), NN) * scale).astype(BF16)
        memory_grad_ref[1, 0, :, kv] = dot(probs.astype(BF16), grad, NN).astype(BF16)


def call(kernel, outs, args, smem=(), scratch=(), **params):
    specs = [pl.BlockSpec(memory_space=pltpu.SMEM if i in smem else pltpu.VMEM) for i in range(len(args))]
    return pl.pallas_call(
        kernel,
        out_shape=outs,
        in_specs=specs,
        out_specs=jax.tree.map(lambda _: pl.BlockSpec(memory_space=pltpu.VMEM), outs),
        scratch_shapes=scratch,
        compiler_params=pltpu.CompilerParams(vmem_limit_bytes=16 * 2**20),
        interpret=INTERPRET,
        **params,
    )(*args)


def sds(shape, dtype=F32):
    return jax.ShapeDtypeStruct(shape, dtype)


INTERPRET = False
SPLIT = (2, 12, 2)
AXES = ("sec", "yh", "z", "core", "mp")
DP = ("yh", "z", "core")
Y = ("sec", "yh")


def in_hbm(x):
    return x if INTERPRET else pltpu.with_memory_space_constraint(x, pltpu.HBM)


def full(x):
    zeros = (0,) * len(x.shape)
    return pl.BlockSpec(x.shape, lambda i: zeros)


def exchange(x, axes):
    return lax.all_to_all(x, axes, 0, 0, tiled=True)


def swap(x, n):
    return lax.ppermute(x, "core", [(i, n - 1 - i) for i in range(n)])


def on_device(policy_query, policy_memory, chosen, adapter_rows, adapter_down, adapter_up,
              scorer_query, scorer_key_values, score_heads, document_ids, prompt_lengths):
    sec = lax.axis_index("sec").astype(jnp.int32).reshape(1)
    core = lax.axis_index("core").astype(jnp.int32).reshape(1)
    n_sec, n_mp = lax.axis_size("sec"), lax.axis_size("mp")
    n_yh, n_z, n_core = (lax.axis_size(a) for a in DP)
    n_y = n_sec * n_yh
    query = policy_query[0]
    rows = chosen[0]
    tokens, features = query.shape
    kv_features = policy_memory.shape[3]
    adapter = adapter_rows[0]
    down = adapter_down.T
    rank = down.shape[0]
    width = adapter.shape[1]
    heads = features // HEAD
    prompts = prompt_lengths[:, 0]
    blocks = (features + width) // HEAD
    half = blocks // n_core * rank
    per = half // n_z

    below = lax.ppermute(rows, "sec", [(1, 0), (2, 1)])
    other = lax.ppermute(rows, "sec", [(2, 0), (0, 1)])
    scorer = pl.pallas_call(
        scorer_kernel,
        grid=(n_sec,),
        out_shape=(sds((n_sec, tokens, features)), sds((tokens, features), BF16)),
        in_specs=[
            pl.BlockSpec((None, 1, tokens), lambda j: (j, 0, 0)),
            pl.BlockSpec((None, None, None, tokens, features), lambda j: (0, j, 0, 0, 0)),
            pl.BlockSpec((None, None, None, None, tokens, kv_features), lambda j: (0, 0, j, 0, 0, 0)),
            pl.BlockSpec((None, None, None, None, tokens, kv_features), lambda j: (0, 1, j, 0, 0, 0)),
        ],
        out_specs=(
            pl.BlockSpec((None, tokens, features), lambda j: (j, 0, 0)),
            pl.BlockSpec((tokens, features), lambda j: (0, 0)),
        ),
        compiler_params=pltpu.CompilerParams(vmem_limit_bytes=16 * 2**20),
        interpret=INTERPRET,
        cost_estimate=pl.CostEstimate(flops=300_000_000, bytes_accessed=8_000_000, transcendentals=600_000),
    )
    pairs = in_hbm(scorer_key_values)
    scorer_att, last = scorer(in_hbm(document_ids), in_hbm(scorer_query), pairs, pairs)
    first = lax.ppermute(last, "sec", [(0, 3)])
    second = lax.ppermute(last, "sec", [(1, 3)])
    held = (document_ids, query, policy_memory, rows, adapter, down, adapter_up)
    groups = heads * HEAD // kv_features
    results = (sds((tokens, features)), sds((heads // groups, tokens, groups * tokens)), sds((2 * rank + 8, tokens)))
    policy = pl.pallas_call(
        policy_kernel,
        grid=(1,),
        out_shape=results,
        in_specs=[pl.BlockSpec(memory_space=pltpu.SMEM)] + [full(x) for x in held] + [pl.BlockSpec(memory_space=pl.ANY)],
        out_specs=tuple(full(x) for x in results),
        compiler_params=pltpu.CompilerParams(vmem_limit_bytes=16 * 2**20),
        interpret=INTERPRET,
        cost_estimate=pl.CostEstimate(flops=150_000_000, bytes_accessed=4_000_000, transcendentals=150_000),
    )
    attended, probs, part = policy(sec, *map(in_hbm, held), last)
    parts = (part,) + tuple(
        lax.ppermute(part, "mp", [(i, (i + k) % n_mp) for i in range(n_mp)]) for k in range(1, n_mp)
    )
    partials = call(score_kernel, sds((n_sec * n_mp, 4, tokens)),
                    (sec, scorer_att, rows, below, other, first, second, score_heads), smem=(0,),
                    cost_estimate=pl.CostEstimate(flops=2_000_000, bytes_accessed=3_000_000, transcendentals=0))
    got = exchange(partials, ("sec", "mp")).reshape(n_sec, n_mp, 4, tokens)
    keep, low_out, own, send = call(
        weights_kernel,
        (sds((8, tokens)), sds((rank, tokens)), sds((2 * half + 8, HEAD)), sds((2 * half + 8, HEAD))),
        (sec, core, prompts, document_ids, got, attended, adapter) + parts,
        smem=(0, 1, 2),
        scratch=(pltpu.VMEM((n_core, 2 * half + 8, HEAD), F32),),
    )
    got = call(pair_kernel, sds((n_z, 2 * per + 16, HEAD), BF16), (own, swap(send, n_core)))
    got = exchange(got, "z")
    got = exchange(call(column_kernel, sds((n_y, 2 * per + 16, HEAD), BF16), (got,)), Y)
    got, moments = call(final_kernel, (sds((n_z, per, HEAD), BF16), sds((8, HEAD))), (got,))
    got = exchange(got, "z")
    got = got.reshape(blocks // n_core, rank, HEAD)
    down_grad, up_grad = call(place_kernel, (sds((rank, features)), sds((rank, width))),
                              (core, got, swap(got, n_core)), smem=(0,),
                              scratch=(pltpu.VMEM((blocks, rank, HEAD), BF16),))
    white, query_grad, memory_grad = call(
        backward_kernel,
        (sds((1, tokens)), sds((tokens, features), BF16), sds(policy_memory.shape, BF16)),
        (moments, keep, low_out, down, rows, probs, query, policy_memory),
        cost_estimate=pl.CostEstimate(flops=300_000_000, bytes_accessed=20_000_000, transcendentals=0),
    )
    return white, query_grad[None], memory_grad, down_grad.T, up_grad


def solution(mesh):
    devices = mesh.devices
    split = SPLIT if int(np.prod(SPLIT)) == devices.shape[1] else (1, devices.shape[1], 1)
    inner = Mesh(devices.reshape((devices.shape[0],) + split + (devices.shape[2],)), AXES)
    both = ("sec",) + DP

    return jax.shard_map(
        on_device,
        mesh=inner,
        in_specs=(
            P(both, None, "mp"),
            P(None, both, None, "mp"),
            P(both, None, "mp"),
            P(both, None, "mp"),
            P("mp", None),
            P(None, "mp"),
            P("sec", None, DP, None, "mp"),
            P("sec", None, None, DP, None, "mp"),
            P(None, "mp"),
            P(None, DP, None),
            P(None, DP, None),
        ),
        out_specs=(
            P(both, None),
            P(both, None, "mp"),
            P(None, both, None, "mp"),
            P("mp", None),
            P(None, "mp"),
        ),
        check_vma=False,
    )
```

```python
import jax
import jax.numpy as jnp
import numpy as np
from jax import lax
from jax.experimental import pallas as pl
from jax.experimental.pallas import tpu as pltpu
from jax.sharding import Mesh, PartitionSpec as P

HEAD = 128
KL = 0.1
DECAY = 0.95
EPS = 1e-05
MASKED = -1e30
SMALL = 2.0 ** -20
F32 = jnp.float32
BF16 = jnp.bfloat16
NT = (((1,), (1,)), ((), ()))
NN = (((1,), (0,)), ((), ()))
TN = (((0,), (0,)), ((), ()))


def dot(a, b, dims):
    return lax.dot_general(a, b, dims, preferred_element_type=F32)


def halves(x):
    high = x.astype(BF16)
    return high, (x - high.astype(F32)).astype(BF16)


def as_column(row):
    n = row.shape[1]
    return jnp.broadcast_to(row, (n, n)).T


def square(row):
    n = row.shape[1]
    return jnp.broadcast_to(row, (n, n))


def kept_of(doc_row, groups):
    n = doc_row.shape[1]
    doc = doc_row.astype(F32)
    rows = lax.broadcasted_iota(jnp.int32, (n, n), 0)
    lanes = lax.broadcasted_iota(jnp.int32, (n, n), 1)
    kept = jnp.where((as_column(doc) == square(doc)) & (rows <= lanes), 1.0, 0.0)
    return jnp.concatenate([kept] * groups, axis=1) > 0.5


def stacked(ref, group, groups):
    first = group * groups
    return jnp.concatenate([ref[:, (first + i) * HEAD:(first + i + 1) * HEAD] for i in range(groups)], axis=0)


def probs_of(query, keys, kept):
    scores = dot(keys, query, NT)
    scores = jnp.where(kept, scores, MASKED)
    top = jnp.max(scores, axis=0, keepdims=True)
    raised = jnp.exp((scores - top) * HEAD ** (-0.5))
    return raised * (1.0 / jnp.sum(raised, axis=0, keepdims=True))


def scorer_kernel(doc_ref, q_ref, k_ref, v_ref, heads_ref, out_ref, last_ref, held_ref):
    n = q_ref.shape[0]
    groups = q_ref.shape[1] // k_ref.shape[1]
    kept = kept_of(doc_ref[...], groups)
    for group in range(k_ref.shape[1] // HEAD):
        kv = slice(group * HEAD, (group + 1) * HEAD)
        probs = probs_of(stacked(q_ref, group, groups), k_ref[:, kv], kept).astype(BF16)
        attended = dot(probs, v_ref[:, kv], TN)
        for i in range(groups):
            at = (group * groups + i) * HEAD
            out_ref[:, at:at + HEAD] = attended[i * n:(i + 1) * n]

    @pl.when(pl.program_id(0) == pl.num_programs(0) - 1)
    def _():
        last_ref[...] = out_ref[...].astype(BF16)
        held_ref[...] = heads_ref[...]


def score_kernel(sec_ref, att_ref, own_ref, next_ref, other_ref, up_ref, first_ref, heads_ref, out_ref):
    sec = sec_ref[0]
    n_sec = att_ref.shape[0]
    copies = out_ref.shape[0] // n_sec
    n_heads = att_ref.shape[2] // HEAD
    late = n_sec - 1

    def score(left, right):
        total = None
        for head in range(n_heads):
            at = slice(head * HEAD, (head + 1) * HEAD)
            term = left(at) * right(at)
            total = term if total is None else total + term
        return jnp.sum(total.T, axis=0, keepdims=True)

    def put(row, index, value):
        for copy in range(copies):
            out_ref[row * copies + copy, index:index + 1] = value

    out_ref[...] = jnp.zeros(out_ref.shape, F32)

    @pl.when(sec < 2)
    def _():
        for held, row in ((own_ref, sec), (next_ref, sec + 1), (other_ref, sec + 2)):
            put(row, 0, score(lambda at: att_ref[row, :, at], lambda at: held[:, at].astype(F32)))

    @pl.when(sec == 1)
    def _():
        put(0, 0, score(lambda at: att_ref[0, :, at], lambda at: up_ref[:, at].astype(F32)))

    @pl.when(sec >= 2)
    def _():
        def weight(at):
            return jnp.where(sec == 2, heads_ref[0:1, at], heads_ref[1:2, at])

        for row in range(n_sec):
            put(row, 0, score(lambda at: att_ref[row, :, at], weight))

    @pl.when(sec == late)
    def _():
        put(late, 1, score(lambda at: first_ref[:, at].astype(F32), lambda at: own_ref[:, at].astype(F32)))


def policy_kernel(sec_ref, doc_ref, q_ref, memory_ref, rows_ref, adapter_ref, down_ref, up_ref, after_ref,
                  att_ref, probs_ref, part_ref):
    del after_ref
    k_ref, v_ref = memory_ref.at[0, 0], memory_ref.at[1, 0]
    n = q_ref.shape[0]
    groups = q_ref.shape[1] // k_ref.shape[1]
    kept = kept_of(doc_ref[sec_ref[0]], groups)
    base = None
    low_in = None
    for group in range(k_ref.shape[1] // HEAD):
        kv = slice(group * HEAD, (group + 1) * HEAD)
        probs = probs_of(stacked(q_ref, group, groups), k_ref[:, kv], kept)
        probs_ref[group] = probs
        attended = dot(probs.astype(BF16), v_ref[:, kv], TN)
        for i in range(groups):
            at = slice((group * groups + i) * HEAD, (group * groups + i + 1) * HEAD)
            own = attended[i * n:(i + 1) * n]
            att_ref[:, at] = own
            term = own * rows_ref[:, at].astype(F32)
            base = term if base is None else base + term
            high, low = halves(own)
            down = down_ref[:, at]
            term = dot(down, high, NT) + dot(down, low, NT)
            low_in = term if low_in is None else low_in + term
    rank = down_ref.shape[0]
    part_ref[0:rank, :] = low_in
    part_ref[rank:2 * rank, :] = dot(up_ref[...], adapter_ref[...], NT)
    base_row = jnp.sum(base.T, axis=0, keepdims=True)
    part_ref[2 * rank:, :] = jnp.broadcast_to(base_row, (8, base_row.shape[1]))


def pick(row, index):
    lane = lax.broadcasted_iota(jnp.int32, row.shape, 1)
    return jnp.sum(jnp.where(lane == index, row, 0.0), axis=1, keepdims=True)


def weights_kernel(sec_ref, core_ref, prompt_ref, doc_ref, got_ref, att_ref, adapter_ref,
                   part0, part1, part2, part3,
                   keep_ref, low_ref, own_ref, send_ref, both_ref):
    sec = sec_ref[0]
    doc = doc_ref[sec].astype(F32)
    n = doc.shape[1]
    doc_col, doc_row = as_column(doc), square(doc)
    rows = lax.broadcasted_iota(jnp.int32, (n, n), 0)
    lanes = lax.broadcasted_iota(jnp.int32, (n, n), 1)
    position = lax.broadcasted_iota(jnp.int32, (1, n), 1).astype(F32)
    start = jnp.sum(jnp.where(doc_col < doc_row, 1.0, 0.0), axis=0, keepdims=True)
    ending = jnp.sum(jnp.where(doc_col <= doc_row, 1.0, 0.0), axis=0, keepdims=True) - 1.0
    prompt = jnp.zeros((1, n), F32)
    for label in range(prompt_ref.shape[1]):
        length = prompt_ref[sec, label].astype(F32)
        prompt = jnp.where(doc == float(label), length, prompt)
    respond = jnp.where(position - start >= prompt, 1.0, 0.0)
    closing = jnp.where(position == ending, 1.0, 0.0)

    def section(index):
        total = jnp.sum(got_ref[index, :, 0, :], axis=0, keepdims=True)
        if index == 0:
            total = total + jnp.sum(got_ref[3, :, 1, :], axis=0, keepdims=True)
        return total

    old, ref, reward, value = section(0), section(1), section(2), section(3)
    next_value = jnp.where(position < n - 1.0, pltpu.roll(value, n - 1, 1), 0.0) * (1.0 - closing)
    delta = -KL * (old - ref) + closing * reward + next_value - value
    later = rows - lanes
    linked = (doc_col == doc_row) & (later >= 0)
    powers = jnp.exp(jnp.maximum(later, 0).astype(F32) * float(np.log(DECAY)))
    terms = jnp.where(linked, powers, 0.0) * as_column(delta)
    advantage = jnp.sum(terms, axis=0, keepdims=True)
    lane = lax.broadcasted_iota(jnp.int32, (1, n), 1)
    count = jnp.sum(respond, axis=1, keepdims=True)
    total = jnp.sum(respond * advantage, axis=1, keepdims=True)
    squares = jnp.sum(respond * advantage * advantage, axis=1, keepdims=True)
    moments = jnp.where(lane == 0, count, jnp.where(lane == 1, total, jnp.where(lane == 2, squares, 0.0)))

    rank = (part0.shape[0] - 8) // 2
    part = (part0[...] + part1[...]) + (part2[...] + part3[...])
    low_in, low_out, base = part[0:rank], part[rank:2 * rank], part[2 * rank:2 * rank + 1]
    policy_new = base + jnp.sum(low_in * low_out, axis=0, keepdims=True)
    weight = -respond * jnp.exp(policy_new - old)
    keep_ref[0:1, :] = respond
    keep_ref[1:2, :] = advantage
    keep_ref[2:3, :] = weight
    keep_ref[3:8, :] = jnp.zeros((5, n), F32)
    low_ref[...] = low_out
    plain = weight * SMALL
    lifted = plain * advantage
    out_high, out_low = halves(jnp.concatenate([plain * low_out, lifted * low_out], axis=0))
    in_high, in_low = halves(jnp.concatenate([plain * low_in, lifted * low_in], axis=0))
    n_down = att_ref.shape[1] // HEAD
    cores = both_ref.shape[0]
    slots = (n_down + adapter_ref.shape[1] // HEAD) // cores
    half = slots * rank
    for block in range(cores * slots):
        if block < n_down:
            high, low = halves(att_ref[:, block * HEAD:(block + 1) * HEAD])
            term = dot(out_high, high, NN) + (dot(out_low, high, NN) + dot(out_high, low, NN))
        else:
            at = (block - n_down) * HEAD
            columns = adapter_ref[:, at:at + HEAD]
            term = dot(in_high, columns, NN) + dot(in_low, columns, NN)
        owner, at = block // slots, block % slots * rank
        both_ref[owner, at:at + rank] = term[0:rank]
        both_ref[owner, half + at:half + at + rank] = term[rank:]
    for owner in range(cores):
        both_ref[owner, 2 * half:] = jnp.broadcast_to(moments, (8, n))
    core = core_ref[0]
    own_ref[...] = both_ref[core]
    send_ref[...] = both_ref[cores - 1 - core]


def middle(moments):
    near = pick(moments, 1) / jnp.maximum(pick(moments, 0), 1.0)
    return near.astype(BF16).astype(F32)


def note(moments, centre):
    n = moments.shape[1]
    first = moments.astype(BF16).astype(F32)
    rest = moments - first
    second = rest.astype(BF16).astype(F32)
    third = rest - second
    lane = lax.broadcasted_iota(jnp.int32, moments.shape, 1)
    first = jnp.where(lane == 3, centre, first)
    row = lax.broadcasted_iota(jnp.int32, (16, n), 0)
    return jnp.where(row == 0, first, jnp.where(row == 1, second, jnp.where(row == 2, third, 0.0))).astype(BF16)


def pair_kernel(own_ref, got_ref, out_ref):
    n_z, per = out_ref.shape[0], (out_ref.shape[1] - 16) // 2
    half = n_z * per
    moments = own_ref[2 * half:2 * half + 1] + got_ref[2 * half:2 * half + 1]
    centre = middle(moments)
    tile = note(moments, centre)
    for slot in range(n_z):
        at = slice(slot * per, (slot + 1) * per)
        to = slice(half + slot * per, half + (slot + 1) * per)
        plain = own_ref[at] + got_ref[at]
        lifted = own_ref[to] + got_ref[to]
        out_ref[slot, 0:per] = plain.astype(BF16)
        out_ref[slot, per:2 * per] = (lifted - centre * plain).astype(BF16)
        out_ref[slot, 2 * per:] = tile


def gathered(got_ref, per):
    notes = [jnp.sum(got_ref[i, 2 * per:].astype(F32), axis=0, keepdims=True) for i in range(got_ref.shape[0])]
    lane = lax.broadcasted_iota(jnp.int32, notes[0].shape, 1)
    moments = notes[0]
    for other in notes[1:]:
        moments = moments + other
    return jnp.where(lane < 3, moments, 0.0), [pick(x, 3) for x in notes]


def added(got_ref, per, centres, centre):
    plain, lifted = None, None
    for index in range(got_ref.shape[0]):
        mine = got_ref[index, 0:per].astype(F32)
        high = got_ref[index, per:2 * per].astype(F32) + (centres[index] - centre) * mine
        plain = mine if plain is None else plain + mine
        lifted = high if lifted is None else lifted + high
    return plain, lifted


def column_kernel(got_ref, out_ref):
    per = (got_ref.shape[1] - 16) // 2
    moments, centres = gathered(got_ref, per)
    centre = middle(moments)
    plain, lifted = added(got_ref, per, centres, centre)
    plain, lifted = plain.astype(BF16), lifted.astype(BF16)
    tile = note(moments, centre)
    for index in range(out_ref.shape[0]):
        out_ref[index, 0:per] = plain
        out_ref[index, per:2 * per] = lifted
        out_ref[index, 2 * per:] = tile


def scale_of(moments):
    count = pick(moments, 0)
    mean = pick(moments, 1) / count
    spread = pick(moments, 2) / count - mean * mean
    return count, mean, lax.rsqrt(spread + EPS)


def final_kernel(got_ref, out_ref, moments_ref):
    per = (got_ref.shape[1] - 16) // 2
    moments, centres = gathered(got_ref, per)
    count, mean, scale = scale_of(moments)
    _, lifted = added(got_ref, per, centres, mean)
    total = (lifted * (scale / count * (1.0 / SMALL))).astype(BF16)
    for index in range(out_ref.shape[0]):
        out_ref[index] = total
    moments_ref[...] = jnp.broadcast_to(moments, moments_ref.shape)


def place_kernel(core_ref, own_ref, other_ref, down_ref, up_ref, both_ref):
    core = core_ref[0]
    slots = own_ref.shape[0]
    cores = both_ref.shape[0] // slots
    for slot in range(slots):
        both_ref[(cores - 1 - core) * slots + slot] = other_ref[slot]
        both_ref[core * slots + slot] = own_ref[slot]
    n_down = down_ref.shape[1] // HEAD
    for block in range(both_ref.shape[0]):
        value = both_ref[block].astype(F32)
        if block < n_down:
            down_ref[:, block * HEAD:(block + 1) * HEAD] = value
        else:
            at = (block - n_down) * HEAD
            up_ref[:, at:at + HEAD] = value


def backward_kernel(moments_ref, keep_ref, low_ref, down_ref, rows_ref, probs_ref, q_ref, memory_ref,
                    white_ref, query_ref, memory_grad_ref):
    k_ref, v_ref = memory_ref.at[0, 0], memory_ref.at[1, 0]
    n = q_ref.shape[0]
    count, mean, inverse = scale_of(moments_ref[0:1, :])
    whitened = keep_ref[0:1, :] * (keep_ref[1:2, :] - mean) * inverse
    white_ref[...] = whitened
    grad_score = keep_ref[2:3, :] * whitened / count
    grad_col = as_column(grad_score)
    high, low = halves(grad_score * low_ref[...])
    groups = q_ref.shape[1] // k_ref.shape[1]
    scale = HEAD ** (-0.5)
    for group in range(k_ref.shape[1] // HEAD):
        kv = slice(group * HEAD, (group + 1) * HEAD)
        keys, values = k_ref[:, kv], v_ref[:, kv]
        grads = []
        for head in range(group * groups, (group + 1) * groups):
            at = slice(head * HEAD, (head + 1) * HEAD)
            down = down_ref[:, at]
            grad = grad_col * rows_ref[:, at].astype(F32) + (dot(high, down, TN) + dot(low, down, TN))
            grads.append(grad.astype(BF16))
        grad = jnp.concatenate(grads, axis=0)
        probs = probs_ref[group]
        dprobs = dot(values, grad, NT)
        inner = jnp.sum(probs * dprobs, axis=0, keepdims=True)
        dscores = (probs * (dprobs - inner)).astype(BF16)
        query_grad = (dot(dscores, keys, TN) * scale).astype(BF16)
        for i in range(groups):
            at = (group * groups + i) * HEAD
            query_ref[:, at:at + HEAD] = query_grad[i * n:(i + 1) * n]
        memory_grad_ref[0, 0, :, kv] = (dot(dscores, stacked(q_ref, group, groups), NN) * scale).astype(BF16)
        memory_grad_ref[1, 0, :, kv] = dot(probs.astype(BF16), grad, NN).astype(BF16)


def call(kernel, outs, args, smem=(), scratch=(), **params):
    specs = [pl.BlockSpec(memory_space=pltpu.SMEM if i in smem else pltpu.VMEM) for i in range(len(args))]
    return pl.pallas_call(
        kernel,
        out_shape=outs,
        in_specs=specs,
        out_specs=jax.tree.map(lambda _: pl.BlockSpec(memory_space=pltpu.VMEM), outs),
        scratch_shapes=scratch,
        compiler_params=pltpu.CompilerParams(vmem_limit_bytes=16 * 2**20),
        interpret=INTERPRET,
        **params,
    )(*args)


def sds(shape, dtype=F32):
    return jax.ShapeDtypeStruct(shape, dtype)


INTERPRET = False
SPLIT = (2, 12, 2)
AXES = ("sec", "yh", "z", "core", "mp")
DP = ("yh", "z", "core")
Y = ("sec", "yh")


def in_hbm(x):
    return x if INTERPRET else pltpu.with_memory_space_constraint(x, pltpu.HBM)


def full(x):
    zeros = (0,) * len(x.shape)
    return pl.BlockSpec(x.shape, lambda i: zeros)


def exchange(x, axes):
    return lax.all_to_all(x, axes, 0, 0, tiled=True)


def swap(x, n):
    return lax.ppermute(x, "core", [(i, n - 1 - i) for i in range(n)])


def on_device(policy_query, policy_memory, chosen, adapter_rows, adapter_down, adapter_up,
              scorer_query, scorer_key_values, score_heads, document_ids, prompt_lengths):
    sec = lax.axis_index("sec").astype(jnp.int32).reshape(1)
    core = lax.axis_index("core").astype(jnp.int32).reshape(1)
    n_sec, n_mp = lax.axis_size("sec"), lax.axis_size("mp")
    n_yh, n_z, n_core = (lax.axis_size(a) for a in DP)
    n_y = n_sec * n_yh
    query = policy_query[0]
    rows = chosen[0]
    tokens, features = query.shape
    kv_features = policy_memory.shape[3]
    adapter = adapter_rows[0]
    down = adapter_down.T
    rank = down.shape[0]
    width = adapter.shape[1]
    heads = features // HEAD
    prompts = prompt_lengths[:, 0]
    blocks = (features + width) // HEAD
    half = blocks // n_core * rank
    per = half // n_z

    below = lax.ppermute(rows, "sec", [(1, 0), (2, 1)])
    other = lax.ppermute(rows, "sec", [(2, 0), (3, 1)])
    up = lax.ppermute(rows, "sec", [(0, 1)])
    scorer = pl.pallas_call(
        scorer_kernel,
        grid=(n_sec,),
        out_shape=(sds((n_sec, tokens, features)), sds((tokens, features), BF16), sds(score_heads.shape)),
        in_specs=[
            pl.BlockSpec((None, 1, tokens), lambda j: (j, 0, 0)),
            pl.BlockSpec((None, None, None, tokens, features), lambda j: (0, j, 0, 0, 0)),
            pl.BlockSpec((None, None, None, None, tokens, kv_features), lambda j: (0, 0, j, 0, 0, 0)),
            pl.BlockSpec((None, None, None, None, tokens, kv_features), lambda j: (0, 1, j, 0, 0, 0)),
            full(score_heads),
        ],
        out_specs=(
            pl.BlockSpec((None, tokens, features), lambda j: (j, 0, 0)),
            pl.BlockSpec((tokens, features), lambda j: (0, 0)),
            full(score_heads),
        ),
        compiler_params=pltpu.CompilerParams(vmem_limit_bytes=16 * 2**20),
        interpret=INTERPRET,
        cost_estimate=pl.CostEstimate(flops=300_000_000, bytes_accessed=8_000_000, transcendentals=600_000),
    )
    pairs = in_hbm(scorer_key_values)
    scorer_att, last, weights = scorer(
        in_hbm(document_ids), in_hbm(scorer_query), pairs, pairs, in_hbm(score_heads))
    first = lax.ppermute(last, "sec", [(0, 3)])
    held = (document_ids, query, policy_memory, rows, adapter, down, adapter_up)
    groups = heads * HEAD // kv_features
    results = (sds((tokens, features)), sds((heads // groups, tokens, groups * tokens)), sds((2 * rank + 8, tokens)))
    policy = pl.pallas_call(
        policy_kernel,
        grid=(1,),
        out_shape=results,
        in_specs=[pl.BlockSpec(memory_space=pltpu.SMEM)] + [full(x) for x in held] + [pl.BlockSpec(memory_space=pl.ANY)],
        out_specs=tuple(full(x) for x in results),
        compiler_params=pltpu.CompilerParams(vmem_limit_bytes=16 * 2**20),
        interpret=INTERPRET,
        cost_estimate=pl.CostEstimate(flops=150_000_000, bytes_accessed=4_000_000, transcendentals=150_000),
    )
    attended, probs, part = policy(sec, *map(in_hbm, held), last)

    def from_mp(k):
        return lax.ppermute(part, "mp", [(i, (i + k) % n_mp) for i in range(n_mp)])

    parts = (part, from_mp(2), from_mp(1))
    parts += (from_mp(3),)
    partials = call(score_kernel, sds((n_sec * n_mp, 4, tokens)),
                    (sec, scorer_att, rows, below, other, up, first, weights), smem=(0,),
                    cost_estimate=pl.CostEstimate(flops=2_000_000, bytes_accessed=3_000_000, transcendentals=0))
    got = exchange(partials, ("sec", "mp"))
    got = got.reshape(n_sec, n_mp, 4, tokens)
    keep, low_out, own, send = call(
        weights_kernel,
        (sds((8, tokens)), sds((rank, tokens)), sds((2 * half + 8, HEAD)), sds((2 * half + 8, HEAD))),
        (sec, core, prompts, document_ids, got, attended, adapter) + parts,
        smem=(0, 1, 2),
        scratch=(pltpu.VMEM((n_core, 2 * half + 8, HEAD), F32),),
    )
    got = call(pair_kernel, sds((n_z, 2 * per + 16, HEAD), BF16), (own, swap(send, n_core)))
    got = exchange(got, "z")
    got = exchange(call(column_kernel, sds((n_y, 2 * per + 16, HEAD), BF16), (got,)), Y)
    got, moments = call(final_kernel, (sds((n_z, per, HEAD), BF16), sds((8, HEAD))), (got,))
    got = exchange(got, "z")
    got = got.reshape(blocks // n_core, rank, HEAD)
    down_grad, up_grad = call(place_kernel, (sds((rank, features)), sds((rank, width))),
                              (core, got, swap(got, n_core)), smem=(0,),
                              scratch=(pltpu.VMEM((blocks, rank, HEAD), BF16),))
    white, query_grad, memory_grad = call(
        backward_kernel,
        (sds((1, tokens)), sds((tokens, features), BF16), sds(policy_memory.shape, BF16)),
        (moments, keep, low_out, down, rows, probs, query, policy_memory),
        cost_estimate=pl.CostEstimate(flops=300_000_000, bytes_accessed=20_000_000, transcendentals=0),
    )
    return white, query_grad[None], memory_grad, down_grad.T, up_grad


def solution(mesh):
    devices = mesh.devices
    split = SPLIT if int(np.prod(SPLIT)) == devices.shape[1] else (1, devices.shape[1], 1)
    inner = Mesh(devices.reshape((devices.shape[0],) + split + (devices.shape[2],)), AXES)
    both = ("sec",) + DP

    return jax.shard_map(
        on_device,
        mesh=inner,
        in_specs=(
            P(both, None, "mp"),
            P(None, both, None, "mp"),
            P(both, None, "mp"),
            P(both, None, "mp"),
            P("mp", None),
            P(None, "mp"),
            P("sec", None, DP, None, "mp"),
            P("sec", None, None, DP, None, "mp"),
            P(None, "mp"),
            P(None, DP, None),
            P(None, DP, None),
        ),
        out_specs=(
            P(both, None),
            P(both, None, "mp"),
            P(None, both, None, "mp"),
            P("mp", None),
            P(None, "mp"),
        ),
        check_vma=False,
    )
```

```python
import jax
import jax.numpy as jnp
import numpy as np
from jax import lax
from jax.experimental import pallas as pl
from jax.experimental.pallas import tpu as pltpu
from jax.sharding import Mesh, PartitionSpec as P

HEAD = 128
KL = 0.1
DECAY = 0.95
EPS = 1e-05
MASKED = -1e30
SMALL = 2.0 ** -20
F32 = jnp.float32
BF16 = jnp.bfloat16
NT = (((1,), (1,)), ((), ()))
NN = (((1,), (0,)), ((), ()))
TN = (((0,), (0,)), ((), ()))


def dot(a, b, dims):
    return lax.dot_general(a, b, dims, preferred_element_type=F32)


def halves(x):
    high = x.astype(BF16)
    return high, (x - high.astype(F32)).astype(BF16)


def as_column(row):
    n = row.shape[1]
    return jnp.broadcast_to(row, (n, n)).T


def square(row):
    n = row.shape[1]
    return jnp.broadcast_to(row, (n, n))


def kept_of(doc_row, groups):
    n = doc_row.shape[1]
    doc = doc_row.astype(F32)
    rows = lax.broadcasted_iota(jnp.int32, (n, n), 0)
    lanes = lax.broadcasted_iota(jnp.int32, (n, n), 1)
    kept = jnp.where((as_column(doc) == square(doc)) & (rows <= lanes), 1.0, 0.0)
    return jnp.concatenate([kept] * groups, axis=1) > 0.5


def stacked(ref, group, groups):
    first = group * groups
    return jnp.concatenate([ref[:, (first + i) * HEAD:(first + i + 1) * HEAD] for i in range(groups)], axis=0)


def probs_of(query, keys, kept):
    scores = dot(keys, query, NT)
    scores = jnp.where(kept, scores, MASKED)
    top = jnp.max(scores, axis=0, keepdims=True)
    raised = jnp.exp((scores - top) * HEAD ** (-0.5))
    return raised * (1.0 / jnp.sum(raised, axis=0, keepdims=True))


def scorer_kernel(sec_ref, doc_ref, q_ref, k_ref, v_ref, heads_ref, out_ref, last_ref, held_ref):
    n = q_ref.shape[0]
    groups = q_ref.shape[1] // k_ref.shape[1]
    kept = kept_of(doc_ref[...], groups)
    for group in range(k_ref.shape[1] // HEAD):
        kv = slice(group * HEAD, (group + 1) * HEAD)
        probs = probs_of(stacked(q_ref, group, groups), k_ref[:, kv], kept).astype(BF16)
        attended = dot(probs, v_ref[:, kv], TN)
        for i in range(groups):
            at = (group * groups + i) * HEAD
            out_ref[:, at:at + HEAD] = attended[i * n:(i + 1) * n]

    n_sec = pl.num_programs(0)

    @pl.when(pl.program_id(0) == lax.rem(sec_ref[0] + n_sec - 1, n_sec))
    def _():
        last_ref[...] = out_ref[...].astype(BF16)

    @pl.when(pl.program_id(0) == 0)
    def _():
        held_ref[...] = heads_ref[...]


def score_kernel(sec_ref, att_ref, own_ref, next_ref, other_ref, first_ref, heads_ref,
                 part_ref, near_ref, out_ref, sum_ref):
    sum_ref[...] = part_ref[...] + near_ref[...]
    sec = sec_ref[0]
    n_sec = att_ref.shape[0]
    copies = out_ref.shape[0] // n_sec
    n_heads = att_ref.shape[2] // HEAD
    late = n_sec - 1

    def score(left, right):
        total = None
        for head in range(n_heads):
            at = slice(head * HEAD, (head + 1) * HEAD)
            term = left(at) * right(at)
            total = term if total is None else total + term
        return jnp.sum(total.T, axis=0, keepdims=True)

    def put(row, index, value):
        for copy in range(copies):
            out_ref[row * copies + copy, index:index + 1] = value

    out_ref[...] = jnp.zeros(out_ref.shape, F32)

    @pl.when(sec < 2)
    def _():
        for held, row in ((own_ref, sec), (next_ref, sec + 1), (other_ref, sec + 2)):
            put(row, 0, score(lambda at: att_ref[row, :, at], lambda at: held[:, at].astype(F32)))

    @pl.when(sec >= 2)
    def _():
        def weight(at):
            return jnp.where(sec == 2, heads_ref[0:1, at], heads_ref[1:2, at])

        for row in range(n_sec):
            put(row, 0, score(lambda at: att_ref[row, :, at], weight))

    @pl.when((sec == late) | (sec == 0))
    def _():
        value = score(lambda at: first_ref[:, at].astype(F32), lambda at: own_ref[:, at].astype(F32))
        put(sec, 1, value)


def policy_kernel(sec_ref, doc_ref, q_ref, memory_ref, rows_ref, adapter_ref, down_ref, up_ref, after_ref,
                  att_ref, held_ref, part_ref):
    held_ref[...] = rows_ref[...]
    del after_ref
    k_ref, v_ref = memory_ref.at[0, 0], memory_ref.at[1, 0]
    n = q_ref.shape[0]
    groups = q_ref.shape[1] // k_ref.shape[1]
    kept = kept_of(doc_ref[sec_ref[0]], groups)
    base = None
    low_in = None
    for group in range(k_ref.shape[1] // HEAD):
        kv = slice(group * HEAD, (group + 1) * HEAD)
        probs = probs_of(stacked(q_ref, group, groups), k_ref[:, kv], kept)
        attended = dot(probs.astype(BF16), v_ref[:, kv], TN)
        for i in range(groups):
            at = slice((group * groups + i) * HEAD, (group * groups + i + 1) * HEAD)
            own = attended[i * n:(i + 1) * n]
            att_ref[:, at] = own
            term = own * rows_ref[:, at].astype(F32)
            base = term if base is None else base + term
            high, low = halves(own)
            down = down_ref[:, at]
            term = dot(down, high, NT) + dot(down, low, NT)
            low_in = term if low_in is None else low_in + term
    rank = down_ref.shape[0]
    part_ref[0:rank, :] = low_in
    part_ref[rank:2 * rank, :] = dot(up_ref[...], adapter_ref[...], NT)
    base_row = jnp.sum(base.T, axis=0, keepdims=True)
    part_ref[2 * rank:, :] = jnp.broadcast_to(base_row, (8, base_row.shape[1]))


def pick(row, index):
    lane = lax.broadcasted_iota(jnp.int32, row.shape, 1)
    return jnp.sum(jnp.where(lane == index, row, 0.0), axis=1, keepdims=True)


def weights_kernel(sec_ref, core_ref, prompt_ref, doc_ref, got_ref, att_ref, adapter_ref,
                   near_ref, far_ref,
                   keep_ref, low_ref, own_ref, send_ref, both_ref):
    sec = sec_ref[0]
    doc = doc_ref[sec].astype(F32)
    n = doc.shape[1]
    doc_col, doc_row = as_column(doc), square(doc)
    rows = lax.broadcasted_iota(jnp.int32, (n, n), 0)
    lanes = lax.broadcasted_iota(jnp.int32, (n, n), 1)
    position = lax.broadcasted_iota(jnp.int32, (1, n), 1).astype(F32)
    start = jnp.sum(jnp.where(doc_col < doc_row, 1.0, 0.0), axis=0, keepdims=True)
    ending = jnp.sum(jnp.where(doc_col <= doc_row, 1.0, 0.0), axis=0, keepdims=True) - 1.0
    prompt = jnp.zeros((1, n), F32)
    for label in range(prompt_ref.shape[1]):
        length = prompt_ref[sec, label].astype(F32)
        prompt = jnp.where(doc == float(label), length, prompt)
    respond = jnp.where(position - start >= prompt, 1.0, 0.0)
    closing = jnp.where(position == ending, 1.0, 0.0)

    def section(index):
        total = jnp.sum(got_ref[index, :, 0, :], axis=0, keepdims=True)
        if index < 2:
            total = total + jnp.sum(got_ref[3 - 3 * index, :, 1, :], axis=0, keepdims=True)
        return total

    old, ref, reward, value = section(0), section(1), section(2), section(3)
    next_value = jnp.where(position < n - 1.0, pltpu.roll(value, n - 1, 1), 0.0) * (1.0 - closing)
    delta = -KL * (old - ref) + closing * reward + next_value - value
    later = rows - lanes
    linked = (doc_col == doc_row) & (later >= 0)
    powers = jnp.exp(jnp.maximum(later, 0).astype(F32) * float(np.log(DECAY)))
    terms = jnp.where(linked, powers, 0.0) * as_column(delta)
    advantage = jnp.sum(terms, axis=0, keepdims=True)
    lane = lax.broadcasted_iota(jnp.int32, (1, n), 1)
    count = jnp.sum(respond, axis=1, keepdims=True)
    total = jnp.sum(respond * advantage, axis=1, keepdims=True)
    squares = jnp.sum(respond * advantage * advantage, axis=1, keepdims=True)
    moments = jnp.where(lane == 0, count, jnp.where(lane == 1, total, jnp.where(lane == 2, squares, 0.0)))

    rank = (near_ref.shape[0] - 8) // 2
    part = near_ref[...] + far_ref[...]
    low_in, low_out, base = part[0:rank], part[rank:2 * rank], part[2 * rank:2 * rank + 1]
    policy_new = base + jnp.sum(low_in * low_out, axis=0, keepdims=True)
    weight = -respond * jnp.exp(policy_new - old)
    keep_ref[0:1, :] = respond
    keep_ref[1:2, :] = advantage
    keep_ref[2:3, :] = weight
    keep_ref[3:8, :] = jnp.zeros((5, n), F32)
    low_ref[...] = low_out
    plain = weight * SMALL
    lifted = plain * advantage
    out_high, out_low = halves(jnp.concatenate([plain * low_out, lifted * low_out], axis=0))
    in_high, in_low = halves(jnp.concatenate([plain * low_in, lifted * low_in], axis=0))
    n_down = att_ref.shape[1] // HEAD
    cores = both_ref.shape[0]
    slots = (n_down + adapter_ref.shape[1] // HEAD) // cores
    half = slots * rank
    for block in range(cores * slots):
        if block < n_down:
            high, low = halves(att_ref[:, block * HEAD:(block + 1) * HEAD])
            term = dot(out_high, high, NN) + (dot(out_low, high, NN) + dot(out_high, low, NN))
        else:
            at = (block - n_down) * HEAD
            columns = adapter_ref[:, at:at + HEAD]
            term = dot(in_high, columns, NN) + dot(in_low, columns, NN)
        owner, at = block // slots, block % slots * rank
        both_ref[owner, at:at + rank] = term[0:rank]
        both_ref[owner, half + at:half + at + rank] = term[rank:]
    for owner in range(cores):
        both_ref[owner, 2 * half:] = jnp.broadcast_to(moments, (8, n))
    core = core_ref[0]
    own_ref[...] = both_ref[core]
    send_ref[...] = both_ref[cores - 1 - core]


def middle(moments):
    near = pick(moments, 1) / jnp.maximum(pick(moments, 0), 1.0)
    return near.astype(BF16).astype(F32)


def note(moments, centre):
    n = moments.shape[1]
    first = moments.astype(BF16).astype(F32)
    rest = moments - first
    second = rest.astype(BF16).astype(F32)
    third = rest - second
    lane = lax.broadcasted_iota(jnp.int32, moments.shape, 1)
    first = jnp.where(lane == 3, centre, first)
    row = lax.broadcasted_iota(jnp.int32, (16, n), 0)
    return jnp.where(row == 0, first, jnp.where(row == 1, second, jnp.where(row == 2, third, 0.0))).astype(BF16)


def pair_kernel(own_ref, got_ref, out_ref):
    n_z, per = out_ref.shape[0], (out_ref.shape[1] - 16) // 2
    half = n_z * per
    moments = own_ref[2 * half:2 * half + 1] + got_ref[2 * half:2 * half + 1]
    centre = middle(moments)
    tile = note(moments, centre)
    for slot in range(n_z):
        at = slice(slot * per, (slot + 1) * per)
        to = slice(half + slot * per, half + (slot + 1) * per)
        plain = own_ref[at] + got_ref[at]
        lifted = own_ref[to] + got_ref[to]
        out_ref[slot, 0:per] = plain.astype(BF16)
        out_ref[slot, per:2 * per] = (lifted - centre * plain).astype(BF16)
        out_ref[slot, 2 * per:] = tile


def gathered(got_ref, per):
    notes = [jnp.sum(got_ref[i, 2 * per:].astype(F32), axis=0, keepdims=True) for i in range(got_ref.shape[0])]
    lane = lax.broadcasted_iota(jnp.int32, notes[0].shape, 1)
    moments = notes[0]
    for other in notes[1:]:
        moments = moments + other
    return jnp.where(lane < 3, moments, 0.0), [pick(x, 3) for x in notes]


def added(got_ref, per, centres, centre):
    plain, lifted = None, None
    for index in range(got_ref.shape[0]):
        both = got_ref[index, 0:2 * per].astype(F32)
        mine = both[0:per]
        high = both[per:2 * per] + (centres[index] - centre) * mine
        plain = mine if plain is None else plain + mine
        lifted = high if lifted is None else lifted + high
    return plain, lifted


def column_kernel(got_ref, out_ref):
    per = (got_ref.shape[1] - 16) // 2
    moments, centres = gathered(got_ref, per)
    centre = middle(moments)
    plain, lifted = added(got_ref, per, centres, centre)
    tile = note(moments, centre)
    part = per // out_ref.shape[0]
    for index in range(out_ref.shape[0]):
        at = slice(index * part, (index + 1) * part)
        out_ref[index, 0:2 * part] = jnp.concatenate([plain[at], lifted[at]], axis=0).astype(BF16)
        out_ref[index, 2 * part:] = tile


def scale_of(moments):
    count = pick(moments, 0)
    mean = pick(moments, 1) / count
    spread = pick(moments, 2) / count - mean * mean
    return count, mean, lax.rsqrt(spread + EPS)


def final_kernel(got_ref, out_ref, moments_ref):
    per = (got_ref.shape[1] - 16) // 2
    moments, centres = gathered(got_ref, per)
    count, mean, scale = scale_of(moments)
    _, lifted = added(got_ref, per, centres, mean)
    total = (lifted * (scale / count * (1.0 / SMALL))).astype(BF16)
    for index in range(out_ref.shape[0]):
        out_ref[index] = total
    moments_ref[...] = jnp.broadcast_to(moments, moments_ref.shape)


def place_kernel(core_ref, own_ref, other_ref, down_ref, up_ref, both_ref):
    core = core_ref[0]
    slots = own_ref.shape[0]
    cores = both_ref.shape[0] // slots
    for slot in range(slots):
        both_ref[(cores - 1 - core) * slots + slot] = other_ref[slot]
        both_ref[core * slots + slot] = own_ref[slot]
    n_down = down_ref.shape[1] // HEAD
    for block in range(both_ref.shape[0]):
        value = both_ref[block].astype(F32)
        if block < n_down:
            down_ref[:, block * HEAD:(block + 1) * HEAD] = value
        else:
            at = (block - n_down) * HEAD
            up_ref[:, at:at + HEAD] = value


def backward_kernel(sec_ref, doc_ref, moments_ref, keep_ref, low_ref, down_ref, rows_ref, q_ref, memory_ref,
                    white_ref, query_ref, memory_grad_ref):
    k_ref, v_ref = memory_ref.at[0, 0], memory_ref.at[1, 0]
    n = q_ref.shape[0]
    count, mean, inverse = scale_of(moments_ref[0:1, :])
    whitened = keep_ref[0:1, :] * (keep_ref[1:2, :] - mean) * inverse
    white_ref[...] = whitened
    grad_score = keep_ref[2:3, :] * whitened / count
    grad_col = as_column(grad_score)
    high, low = halves(grad_score * low_ref[...])
    groups = q_ref.shape[1] // k_ref.shape[1]
    scale = HEAD ** (-0.5)
    kept = kept_of(doc_ref[sec_ref[0]], groups)
    for group in range(k_ref.shape[1] // HEAD):
        kv = slice(group * HEAD, (group + 1) * HEAD)
        keys, values = k_ref[:, kv], v_ref[:, kv]
        grads = []
        for head in range(group * groups, (group + 1) * groups):
            at = slice(head * HEAD, (head + 1) * HEAD)
            down = down_ref[:, at]
            grad = grad_col * rows_ref[:, at].astype(F32) + (dot(high, down, TN) + dot(low, down, TN))
            grads.append(grad.astype(BF16))
        grad = jnp.concatenate(grads, axis=0)
        query = stacked(q_ref, group, groups)
        probs = probs_of(query, keys, kept)
        dprobs = dot(values, grad, NT)
        inner = jnp.sum(probs * dprobs, axis=0, keepdims=True)
        dscores = (probs * (dprobs - inner)).astype(BF16)
        query_grad = (dot(dscores, keys, TN) * scale).astype(BF16)
        for i in range(groups):
            at = (group * groups + i) * HEAD
            query_ref[:, at:at + HEAD] = query_grad[i * n:(i + 1) * n]
        memory_grad_ref[0, 0, :, kv] = (dot(dscores, query, NN) * scale).astype(BF16)
        memory_grad_ref[1, 0, :, kv] = dot(probs.astype(BF16), grad, NN).astype(BF16)


def call(kernel, outs, args, smem=(), scratch=(), **params):
    specs = [pl.BlockSpec(memory_space=pltpu.SMEM if i in smem else pltpu.VMEM) for i in range(len(args))]
    return pl.pallas_call(
        kernel,
        out_shape=outs,
        in_specs=specs,
        out_specs=jax.tree.map(lambda _: pl.BlockSpec(memory_space=pltpu.VMEM), outs),
        scratch_shapes=scratch,
        compiler_params=pltpu.CompilerParams(vmem_limit_bytes=16 * 2**20),
        interpret=INTERPRET,
        **params,
    )(*args)


def sds(shape, dtype=F32):
    return jax.ShapeDtypeStruct(shape, dtype)


INTERPRET = False
SPLIT = (2, 12, 2)
AXES = ("sec", "yh", "z", "core", "mp")
DP = ("yh", "z", "core")
Y = ("sec", "yh")


def in_hbm(x):
    return x if INTERPRET else pltpu.with_memory_space_constraint(x, pltpu.HBM)


def full(x):
    zeros = (0,) * len(x.shape)
    return pl.BlockSpec(x.shape, lambda i: zeros)


def exchange(x, axes):
    return lax.all_to_all(x, axes, 0, 0, tiled=True)


def swap(x, n):
    return lax.ppermute(x, "core", [(i, n - 1 - i) for i in range(n)])


def on_device(policy_query, policy_memory, chosen, adapter_rows, adapter_down, adapter_up,
              scorer_query, scorer_key_values, score_heads, document_ids, prompt_lengths):
    sec = lax.axis_index("sec").astype(jnp.int32).reshape(1)
    core = lax.axis_index("core").astype(jnp.int32).reshape(1)
    n_sec, n_mp = lax.axis_size("sec"), lax.axis_size("mp")
    n_yh, n_z, n_core = (lax.axis_size(a) for a in DP)
    n_y = n_sec * n_yh
    query = policy_query[0]
    rows = chosen[0]
    tokens, features = query.shape
    kv_features = policy_memory.shape[3]
    adapter = adapter_rows[0]
    down = adapter_down.T
    rank = down.shape[0]
    width = adapter.shape[1]
    prompts = prompt_lengths[:, 0]
    blocks = (features + width) // HEAD
    half = blocks // n_core * rank
    per = half // n_y

    below = lax.ppermute(rows, "sec", [(1, 0), (2, 1)])
    other = lax.ppermute(rows, "sec", [(2, 0), (3, 1)])
    scorer = pl.pallas_call(
        scorer_kernel,
        grid=(n_sec,),
        out_shape=(sds((n_sec, tokens, features)), sds((tokens, features), BF16), sds(score_heads.shape)),
        in_specs=[
            pl.BlockSpec(memory_space=pltpu.SMEM),
            pl.BlockSpec((None, 1, tokens), lambda j: (j, 0, 0)),
            pl.BlockSpec((None, None, None, tokens, features), lambda j: (0, j, 0, 0, 0)),
            pl.BlockSpec((None, None, None, None, tokens, kv_features), lambda j: (0, 0, j, 0, 0, 0)),
            pl.BlockSpec((None, None, None, None, tokens, kv_features), lambda j: (0, 1, j, 0, 0, 0)),
            full(score_heads),
        ],
        out_specs=(
            pl.BlockSpec((None, tokens, features), lambda j: (j, 0, 0)),
            pl.BlockSpec((tokens, features), lambda j: (0, 0)),
            full(score_heads),
        ),
        compiler_params=pltpu.CompilerParams(vmem_limit_bytes=16 * 2**20),
        interpret=INTERPRET,
        cost_estimate=pl.CostEstimate(flops=300_000_000, bytes_accessed=8_000_000, transcendentals=600_000),
    )
    pairs = in_hbm(scorer_key_values)
    scorer_att, last, weights = scorer(
        sec, in_hbm(document_ids), in_hbm(scorer_query), pairs, pairs, in_hbm(score_heads))
    first = lax.ppermute(last, "sec", [(0, 3), (1, 0)])
    held = (document_ids, query, policy_memory, rows, adapter, down, adapter_up)
    results = (sds((tokens, features)), sds((tokens, features), BF16), sds((2 * rank + 8, tokens)))
    policy = pl.pallas_call(
        policy_kernel,
        grid=(1,),
        out_shape=results,
        in_specs=[pl.BlockSpec(memory_space=pltpu.SMEM)] + [full(x) for x in held] + [pl.BlockSpec(memory_space=pl.ANY)],
        out_specs=tuple(full(x) for x in results),
        compiler_params=pltpu.CompilerParams(vmem_limit_bytes=16 * 2**20),
        interpret=INTERPRET,
        cost_estimate=pl.CostEstimate(flops=150_000_000, bytes_accessed=4_000_000, transcendentals=150_000),
    )
    attended, rows_held, part = policy(sec, *map(in_hbm, held), last)
    near = lax.ppermute(part, "mp", [(0, 1), (1, 0), (2, 3), (3, 2)])
    partials, near = call(score_kernel, (sds((n_sec * n_mp, 4, tokens)), sds(part.shape)),
                    (sec, scorer_att, rows_held, below, other, first, weights, part, near), smem=(0,),
                    cost_estimate=pl.CostEstimate(flops=2_000_000, bytes_accessed=3_000_000, transcendentals=0))
    got = exchange(partials, ("sec", "mp"))
    got = got.reshape(n_sec, n_mp, 4, tokens)
    far = lax.ppermute(near, "mp", [(0, 3), (3, 0), (1, 2), (2, 1)])
    keep, low_out, own, send = call(
        weights_kernel,
        (sds((8, tokens)), sds((rank, tokens)), sds((2 * half + 8, HEAD)), sds((2 * half + 8, HEAD))),
        (sec, core, prompts, document_ids, got, attended, adapter, near, far),
        smem=(0, 1, 2),
        scratch=(pltpu.VMEM((n_core, 2 * half + 8, HEAD), F32),),
    )
    got = call(pair_kernel, sds((n_y, 2 * per + 16, HEAD), BF16), (own, swap(send, n_core)))
    got = exchange(got, Y)
    part = per // n_z
    got = exchange(call(column_kernel, sds((n_z, 2 * part + 16, HEAD), BF16), (got,)), "z")
    got, moments = call(final_kernel, (sds((n_z, part, HEAD), BF16), sds((8, HEAD))), (got,))
    got = exchange(got, "z")
    got = exchange(jnp.broadcast_to(got.reshape(1, per, HEAD), (n_y, per, HEAD)), Y)
    got = got.reshape(blocks // n_core, rank, HEAD)
    down_grad, up_grad = call(place_kernel, (sds((rank, features)), sds((rank, width))),
                              (core, got, swap(got, n_core)), smem=(0,),
                              scratch=(pltpu.VMEM((blocks, rank, HEAD), BF16),))
    white, query_grad, memory_grad = call(
        backward_kernel,
        (sds((1, tokens)), sds((tokens, features), BF16), sds(policy_memory.shape, BF16)),
        (sec, document_ids, moments, keep, low_out, down, rows, query, policy_memory),
        smem=(0,),
        cost_estimate=pl.CostEstimate(flops=300_000_000, bytes_accessed=20_000_000, transcendentals=0),
    )
    return white, query_grad[None], memory_grad, down_grad.T, up_grad


def solution(mesh):
    devices = mesh.devices
    split = SPLIT if int(np.prod(SPLIT)) == devices.shape[1] else (1, devices.shape[1], 1)
    inner = Mesh(devices.reshape((devices.shape[0],) + split + (devices.shape[2],)), AXES)
    both = ("sec",) + DP

    return jax.shard_map(
        on_device,
        mesh=inner,
        in_specs=(
            P(both, None, "mp"),
            P(None, both, None, "mp"),
            P(both, None, "mp"),
            P(both, None, "mp"),
            P("mp", None),
            P(None, "mp"),
            P("sec", None, DP, None, "mp"),
            P("sec", None, None, DP, None, "mp"),
            P(None, "mp"),
            P(None, DP, None),
            P(None, DP, None),
        ),
        out_specs=(
            P(both, None),
            P(both, None, "mp"),
            P(None, both, None, "mp"),
            P("mp", None),
            P(None, "mp"),
        ),
        check_vma=False,
    )
```
